512 devices in a mesh: grp: 8 (over x, core), path: 64 (over z, y).
Axes of the slice: x: 4, y: 4, z: 16, core: 2. Of those that a mesh axis runs over, the one named last changes fastest.
Arguments:
- normals: float32 [32, 8388608], P(None, ('grp', 'path')), may hold values from -10.1 to 10.1
- spot_today: float32 [32], replicated, may hold values from 0.5 to 2
- volatility: float32 [32], replicated, may hold values from 0.1 to 0.5
- weights: float32 [32], replicated, may hold values from 0.5 to 1.5
- cash_flows: float32 [8388608], P(('grp', 'path')), may hold values from -300 to 300
- exercise: int32 [8388608], P(('grp', 'path')), may hold values 0 or 1
Outputs:
- path_value: float32 [8388608], P(('grp', 'path'))
- state_cot: float32 [32, 8388608], P(None, ('grp', 'path'))
- flow_cot: float32 [8388608], P(('grp', 'path'))
- greeks: float32 [2, 32], replicated
The draws below stay inside these ranges and needn't reach their ends.
All inputs are finite; a program needn't handle non-finite values. No bound on the sum of `exercise` on one device may be relied on, other than what follows from the above.
Results may differ from the reference program's by a relative error of at most 0.0003.
Values sent between devices are 32-bit elements; how exact they have to be, the bound alone decides.
A program may use at most 64 MiB of HBM per device.

```python
import math
import jax
import jax.numpy as jnp
from jax import lax

ASSETS = 32
PATHS = 8388608


def driving(key):
    base_key = jax.random.fold_in(key, 101)
    rough_key = jax.random.fold_in(key, 102)
    common_key = jax.random.fold_in(key, 104)
    base = jax.random.truncated_normal(base_key, -4.0, 4.0, (ASSETS, PATHS), jnp.float32)
    common = jax.random.truncated_normal(common_key, -4.0, 4.0, (PATHS,), jnp.float32)
    mixed = jnp.clip(0.6 * common[None, :] + 0.8 * base, -4.0, 4.0)
    position = jnp.arange(PATHS, dtype=jnp.float32) / PATHS
    rise = 0.6 * jnp.exp(math.log(3.0) * position)
    rough = jnp.exp(jax.random.uniform(rough_key, (PATHS,), jnp.float32, math.log(0.7), math.log(1.4)))
    return mixed * (rise * rough)[None, :]


def draw_normals(key, part):
    return driving(key)


def draw_cash_flows(key, part):
    moves = driving(key)
    noise = 0.5 * jax.random.truncated_normal(jax.random.fold_in(key, 103), -4.0, 4.0, (PATHS,), jnp.float32)
    neighbour = moves * jnp.roll(moves, -1, axis=0)
    signal = jnp.sum(0.5 * moves + 0.3 / math.sqrt(2.0) * (moves * moves - 1.0) + 0.2 * neighbour, axis=0) / math.sqrt(ASSETS)
    return signal + noise


def set_ends(array, rng, smallest, largest):
    longest = array.shape.index(max(array.shape))
    spots = []
    for shift in (0, 1):
        where = [jax.random.randint(jax.random.fold_in(rng, axis), (), 0, length) for axis, length in enumerate(array.shape)]
        where[longest] = (where[longest] + shift) % array.shape[longest]
        spots.append(tuple(where))
    return array.at[spots[0]].set(smallest).at[spots[1]].set(largest)


def setup_inputs(seed: int = 0) -> dict:
    key_of = jax.random.split(jax.random.key(seed), 7)
    return {
        "normals": draw_normals(jax.random.fold_in(key_of[6], 71), 0),
        "spot_today": jnp.clip(jnp.exp(jax.random.uniform(key_of[1], (ASSETS,), jnp.float32, math.log(0.5), math.log(2.0))), 0.5, 2.0),
        "volatility": jnp.clip(jnp.exp(jax.random.uniform(key_of[2], (ASSETS,), jnp.float32, math.log(0.1), math.log(0.5))), 0.1, 0.5),
        "weights": jnp.clip(jax.random.uniform(key_of[3], (ASSETS,), jnp.float32, 0.5, 1.5), 0.5, 1.5),
        "cash_flows": draw_cash_flows(jax.random.fold_in(key_of[6], 71), 0),
        "exercise": set_ends((jax.random.randint(key_of[5], (PATHS,), 0, 20) < 1).astype(jnp.int32), jax.random.fold_in(key_of[5], 1), 0, 1),
    }


expiry_time = 0.5
root_time = math.sqrt(0.5)
inv_root_two = 1.0 / math.sqrt(2.0)
notional = 20.0
soft_width = 0.02

def path_state(normals, spot_today, volatility):
    return spot_today[:, None] * jnp.exp(volatility[:, None] * (root_time * normals) - 0.5 * expiry_time * volatility[:, None] ** 2)

def basis_rows(state, spot_today, volatility):
    scaled = (state / spot_today[:, None] - 1.0) / (volatility[:, None] * root_time)
    leading = jnp.ones_like(scaled[:1])
    squares = (scaled * scaled - 1.0) * inv_root_two
    neighbour = scaled * jnp.roll(scaled, -1, axis=0)
    bounded = jnp.tanh(scaled[:-1])
    return jnp.concatenate([leading, scaled, squares, neighbour, bounded], axis=0)

def payoff(state, spot_today, weights):
    basket = lax.optimization_barrier(jnp.sum(weights[:, None] * state, axis=0)) / jnp.sum(weights * spot_today)
    return notional * soft_width * jax.nn.softplus((basket - 1.0) / soft_width)

def chol_solve(factor, rhs):
    first = lax.linalg.triangular_solve(factor, rhs, left_side=True, lower=True)
    return lax.linalg.triangular_solve(factor, first, left_side=True, lower=True, transpose_a=True)

def reference(normals, spot_today, volatility, weights, cash_flows, exercise):
    assets, paths = normals.shape
    features = 4 * assets
    block_width = math.gcd(paths, 65536)
    block_count = paths // block_width
    highest = lax.Precision.HIGHEST
    contract_last = (((1,), (1,)), ((), ()))

    def block_inputs(block_index):
        block_start = block_index * block_width
        draw_block = lax.dynamic_slice_in_dim(normals, block_start, block_width, 1)
        flow_block = lax.dynamic_slice_in_dim(cash_flows, block_start, block_width, 0)
        taken_flag = lax.dynamic_slice_in_dim(exercise, block_start, block_width, 0).astype(jnp.float32)
        return (draw_block, flow_block, taken_flag)

    def gram_step(running, block_index):
        gram_acc, moment_acc = running
        draw_block, flow_block, taken_flag = block_inputs(block_index)
        basis_block = basis_rows(path_state(draw_block, spot_today, volatility), spot_today, volatility)
        gram_acc = gram_acc + lax.dot_general(basis_block.astype(jnp.float32), basis_block.astype(jnp.float32), contract_last, precision=highest, preferred_element_type=jnp.float32)
        targets = jnp.stack([flow_block, 1.0 - taken_flag])
        moment_acc = moment_acc + lax.dot_general(targets.astype(jnp.float32), basis_block.astype(jnp.float32), contract_last, precision=highest, preferred_element_type=jnp.float32)
        return ((gram_acc, moment_acc), None)
    start_sums = (jnp.zeros((features, features), jnp.float32), jnp.zeros((2, features), jnp.float32))
    (gram_acc, moment_acc), _ = lax.scan(gram_step, start_sums, jnp.arange(block_count, dtype=jnp.int32))
    gram_mean = gram_acc / paths
    moment_mean = moment_acc / paths
    factor = jnp.linalg.cholesky(gram_mean)
    coefficients = chol_solve(factor, moment_mean.T)
    regression = coefficients[:, 0]
    multiplier = coefficients[:, 1]
    coef_rows = coefficients.T

    def adjoint_block(block_index):
        draw_block, flow_block, taken_flag = block_inputs(block_index)
        state, path_back = jax.vjp(lambda spot_level, spread: path_state(draw_block, spot_level, spread), spot_today, volatility)
        (basis_block, reward), feature_back = jax.vjp(lambda current, spot_level, spread: (basis_rows(current, spot_level, spread), payoff(current, spot_level, weights)), state, spot_today, volatility)
        fitted = lax.dot_general(coef_rows.astype(jnp.float32), basis_block.astype(jnp.float32), (((1,), (0,)), ((), ())), precision=highest, preferred_element_type=jnp.float32)
        continuation = fitted[0]
        lam_phi = fitted[1]
        value_block = taken_flag * reward + (1.0 - taken_flag) * continuation
        rows_bar = multiplier[:, None] * (flow_block - continuation)[None, :] + regression[:, None] * (1.0 - taken_flag - lam_phi)[None, :]
        state_bar, spot_bar, spread_bar = feature_back((rows_bar, taken_flag))
        spot_path, spread_path = path_back(state_bar)
        greek_part = jnp.stack([spot_bar + spot_path, spread_bar + spread_path])
        return (value_block, state_bar, lam_phi, greek_part)
    value_blocks, state_blocks, flow_blocks, greek_parts = lax.map(adjoint_block, jnp.arange(block_count, dtype=jnp.int32))
    path_value = value_blocks.reshape(paths)
    state_cot = jnp.transpose(state_blocks, (1, 0, 2)).reshape(assets, paths)
    flow_cot = flow_blocks.reshape(paths)
    greeks = lax.optimization_barrier(jnp.sum(greek_parts, axis=0)) / paths
    return (path_value, state_cot, flow_cot, greeks)
```

```python
import functools
import math

import jax
import jax.numpy as jnp
from jax import lax
from jax.experimental import pallas as pl
from jax.experimental.pallas import tpu as pltpu
from jax.sharding import PartitionSpec as P

MESH = pl.DeviceIdType.MESH
F32, BF16 = jnp.float32, jnp.bfloat16
expiry_time = 0.5
root_time = math.sqrt(0.5)
inv_root_two = 1.0 / math.sqrt(2.0)
root_two = math.sqrt(2.0)
notional = 20.0
soft_width = 0.02
LAST = (((1,), (1,)), ((), ()))
A = 32
N = 4 * A
GSLOTS = 9
SLOTS = 30


def column(row, size):
    eye = lax.broadcasted_iota(jnp.int32, (size, size), 0) == lax.broadcasted_iota(
        jnp.int32, (size, size), 1
    )
    return jnp.sum(jnp.where(eye, jnp.broadcast_to(row, (size, size)), 0.0), axis=1, keepdims=True)


def split(x):
    hi = x.astype(BF16)
    return hi, (x - hi.astype(F32)).astype(BF16)


def solve(g, b):
    lane = lax.broadcasted_iota(jnp.int32, (8, N), 1)
    rows = [g[8 * i : 8 * i + 8, :] for i in range(N // 8)] + [b]
    for k in range(0, N, 4):
        tile = rows[k // 8]
        pivot = []
        for q in range(4):
            r = k % 8 + q
            pivot.append(jnp.broadcast_to(tile[r : r + 1, :], (8, N)))

        def at(i, j):
            return jnp.broadcast_to(pivot[i][:, k + j : k + j + 1], (8, N))

        a, h, c = at(0, 0), at(0, 1), at(1, 1)
        b00, b01, b10, b11 = at(0, 2), at(0, 3), at(1, 2), at(1, 3)
        d00, d01, d11 = at(2, 2), at(2, 3), at(3, 3)
        inv = 1.0 / (a * c - h * h)
        i00, i01, i11 = c * inv, -(h * inv), a * inv
        e00, e01 = i00 * b00 + i01 * b10, i00 * b01 + i01 * b11
        e10, e11 = i01 * b00 + i11 * b10, i01 * b01 + i11 * b11
        s00 = d00 - (b00 * e00 + b10 * e10)
        s01 = d01 - (b00 * e01 + b10 * e11)
        s11 = d11 - (b01 * e01 + b11 * e11)
        inv = 1.0 / (s00 * s11 - s01 * s01)
        w00, w01, w11 = s11 * inv, -(s01 * inv), s00 * inv
        r0, r1, r2, r3 = (pivot[q] - (lane == k + q).astype(F32) for q in range(4))
        t2 = r2 - (e00 * r0 + e10 * r1)
        t3 = r3 - (e01 * r0 + e11 * r1)
        low0 = w00 * t2 + w01 * t3
        low1 = w01 * t2 + w11 * t3
        up0 = (i00 * r0 + i01 * r1) - (e00 * low0 + e01 * low1)
        up1 = (i01 * r0 + i11 * r1) - (e10 * low0 + e11 * low1)
        first = k // 8 if k % 8 == 0 else k // 8 + 1
        for i in range(first, N // 8 + 1):
            x = rows[i]
            c0, c1, c2, c3 = (jnp.broadcast_to(x[:, k + q : k + q + 1], (8, N)) for q in range(4))
            rows[i] = x - ((c0 * up0 + c1 * up1) + (c2 * low0 + c3 * low1))
    return rows[N // 8]


def first_kernel(
    dims, total_paths, width,
    z_hbm, spot_ref, vol_ref, wei_ref, cf_ref, ex_ref,
    s_out, t_out, rew_out, bar_out, coef_out, greek_out,
    z_ref, s_ref, t_ref, f_ref, tar_ref, q_ref,
    acc, acct, accm, accmt, accd, accv,
    pay, recv, zrecv, total,
    in_sem, out_sem, rs_send, rs_recv, z_send, z_recv, ag_send, ag_recv,
):
    local = z_ref.shape[1]
    chunks = local // width
    comm = dims is not None
    if comm:
        nx, ncore, ny, nz = dims
        plane = nx * ncore * ny
        grp, path = lax.axis_index("grp"), lax.axis_index("path")
        my_z, my_y = path // ny, path % ny
        my_x, my_core = grp // ncore, grp % ncore
        me = (my_core * ny + my_y) * nx + my_x

        def place(slot, z):
            x, y, core = slot % nx, (slot // nx) % ny, slot // (nx * ny)
            return (x * ncore + core, z * ny + y)

        barrier = pltpu.get_barrier_semaphore()

        def greet_z(d, carry):
            peer = place(me, (my_z + d) % nz)
            pl.semaphore_signal(barrier, inc=1, device_id=peer, device_id_type=MESH)
            return carry

        def greet_plane(d, carry):
            peer = place((me + d) % plane, my_z)
            pl.semaphore_signal(barrier, inc=1, device_id=peer, device_id_type=MESH)
            return carry

        lax.fori_loop(1, nz, greet_z, 0)
        lax.fori_loop(1, plane, greet_plane, 0)

    def in_copy(c):
        at = pl.ds(pl.multiple_of(c * width, width), width)
        return pltpu.make_async_copy(z_hbm.at[:, at], z_ref.at[:, at], in_sem.at[c])

    def out_copies(c):
        at = pl.ds(pl.multiple_of(c * width, width), width)
        return (
            pltpu.make_async_copy(s_ref.at[:, at], s_out.at[:, at], out_sem.at[0, c]),
            pltpu.make_async_copy(t_ref.at[:, at], t_out.at[:, at], out_sem.at[1, c]),
        )

    for c in range(chunks):
        in_copy(c).start()

    vol = column(vol_ref[...], A)
    spot = column(spot_ref[...], A)
    weight = column(wei_ref[...], A)
    spread = vol * root_time
    half = 0.5 * expiry_time * (vol * vol)
    inv_spread = 1.0 / spread
    inv_vol = 1.0 / vol
    whole = jnp.sum(weight * spot, axis=0, keepdims=True)
    share = weight * spot / whole
    row = lax.broadcasted_iota(jnp.int32, (A, width), 0)
    trow = lax.broadcasted_iota(jnp.int32, (16, width), 0)

    acc[...] = jnp.zeros_like(acc)
    acct[...] = jnp.zeros_like(acct)

    def gram_step(c, carry):
        at = pl.ds(pl.multiple_of(c * width, width), width)
        in_copy(c).wait()
        e = jnp.exp(spread * z_ref[:, at] - half)
        s = (e - 1.0) * inv_spread
        t = jnp.where(row == A - 1, 1.0, jnp.tanh(s))
        s_ref[:, at] = s
        t_ref[:, at] = t
        blocks = (s, (s * s - 1.0) * inv_root_two, s * pltpu.roll(s, A - 1, 0), t)
        for i, x in enumerate(blocks):
            hi, lo = split(x)
            f_ref[i * A : (i + 1) * A, at] = hi
            f_ref[N + i * A : N + (i + 1) * A, at] = lo
        f = f_ref[:, at]
        acc[...] += lax.dot_general(f, f, LAST, preferred_element_type=F32)
        cf = jnp.broadcast_to(cf_ref[:, at], (16, width))
        free = 1.0 - jnp.broadcast_to(ex_ref[:, at], (16, width)).astype(F32)
        c0 = cf.astype(BF16).astype(F32)
        c1 = (cf - c0).astype(BF16).astype(F32)
        c2 = cf - c0 - c1
        targets = jnp.where(
            trow == 0, c0, jnp.where(trow == 1, c1, jnp.where(trow == 2, c2, jnp.where(trow == 3, free, 0.0)))
        ).astype(BF16)
        tar_ref[:, at] = targets
        acct[...] += lax.dot_general(targets, f, LAST, preferred_element_type=F32)
        for copy in out_copies(c):
            copy.start()
        return carry

    lax.fori_loop(0, chunks, gram_step, 0)

    gram = (acc[:N, :N] + (acc[:N, N:] + acc[N:, :N])) + acc[N:, N:]
    moment = acct[:, :N] + acct[:, N:]
    lane = lax.broadcasted_iota(jnp.int32, (N // 2, N), 1)
    prow = lax.broadcasted_iota(jnp.int32, (N // 2, N), 0)
    corner = pltpu.roll(gram[N // 2 :, :], N // 2, 1)
    packed = jnp.where(lane < prow, corner, gram[: N // 2, :])
    diagonal = jnp.sum(jnp.where(lane == prow, corner, 0.0), axis=0, keepdims=True)
    for j in range(8):
        pay[j] = packed[8 * j : 8 * j + 8, :]
    r8 = lax.broadcasted_iota(jnp.int32, (8, N), 0)
    pay[8] = jnp.where(
        r8 == 0,
        moment[0:1, :] + moment[1:2, :] + moment[2:3, :],
        jnp.where(r8 == 1, moment[3:4, :], jnp.where(r8 == 2, diagonal, 0.0)),
    )

    def rs_copy(slot):
        return pltpu.make_async_remote_copy(
            src_ref=pay.at[slot], dst_ref=recv.at[me], send_sem=rs_send.at[slot], recv_sem=rs_recv.at[me],
            device_id=place(slot, my_z), device_id_type=MESH,
        )

    def rs_start(low, high):
        for slot in range(low, high):
            @pl.when(me != slot)
            def _():
                rs_copy(slot).start()

            @pl.when(me == slot)
            def _():
                recv[me] = pay[slot]

    def arrived(buffer, sem, i):
        return pltpu.make_async_remote_copy(
            src_ref=buffer.at[i], dst_ref=buffer.at[i], send_sem=rs_send.at[0], recv_sem=sem.at[i],
            device_id=place(me, my_z), device_id_type=MESH,
        )

    def z_copy(d):
        return pltpu.make_async_remote_copy(
            src_ref=zrecv.at[my_z], dst_ref=zrecv.at[my_z], send_sem=z_send.at[d], recv_sem=z_recv.at[my_z],
            device_id=place(me, (my_z + d) % nz), device_id_type=MESH,
        )

    def ag_copy(d):
        return pltpu.make_async_remote_copy(
            src_ref=total.at[me], dst_ref=total.at[me], send_sem=ag_send.at[d], recv_sem=ag_recv.at[me],
            device_id=place((me + d) % plane, my_z), device_id_type=MESH,
        )

    def z_stage():
        def wait(d, carry):
            arrived(recv, rs_recv, (me + d) % plane).wait_recv()
            return carry

        lax.fori_loop(1, plane, wait, 0)
        parts = [recv[i] for i in range(plane)]
        while len(parts) > 1:
            parts = [parts[i] + parts[i + 1] for i in range(0, len(parts), 2)]
        zrecv[my_z] = parts[0]
        for i in range(nz // 2):
            for d in ((nz // 2,) if i == 0 else (nz // 2 - i, nz // 2 + i)):
                z_copy(d).start()

    def ag_stage():
        def wait(d, carry):
            arrived(zrecv, z_recv, (my_z + d) % nz).wait_recv()
            return carry

        lax.fori_loop(1, nz, wait, 0)
        parts = [zrecv[i] for i in range(nz)]
        while len(parts) > 1:
            parts = [parts[i] + parts[i + 1] for i in range(0, len(parts), 2)]
        total[me] = parts[0]

        def send(d, carry):
            ag_copy(d).start()
            return carry

        lax.fori_loop(1, plane, send, 0)

    def ag_wait(low, high):
        def wait(slot, carry):
            @pl.when(me != slot)
            def _():
                arrived(total, ag_recv, slot).wait_recv()

            return carry

        lax.fori_loop(low, high, wait, 0)

    owns_gram = owns_rest = None
    if comm:
        owns_gram = me < GSLOTS
        owns_rest = jnp.logical_and(me >= GSLOTS, me < SLOTS)
        pl.semaphore_wait(barrier, nz - 1 + plane - 1)
        rs_start(0, GSLOTS)

    accm[...] = jnp.zeros_like(accm)
    accmt[...] = jnp.zeros_like(accmt)
    accd[...] = jnp.zeros_like(accd)
    accv[...] = jnp.zeros_like(accv)

    def adjoint_step(c, carry):
        at = pl.ds(pl.multiple_of(c * width, width), width)
        s, t = s_ref[:, at], t_ref[:, at]
        e = 1.0 + s * spread
        drift = e * (z_ref[:, at] - spread)
        q = (drift - s) * inv_vol
        for i, x in enumerate(
            (q, q * s, q * pltpu.roll(s, A - 1, 0), q * pltpu.roll(s, 1, 0), q * (1.0 - t * t))
        ):
            hi, lo = split(x)
            q_ref[i * A : (i + 1) * A, :] = hi
            q_ref[(5 + i) * A : (6 + i) * A, :] = lo
        qs = q_ref[...]
        accm[...] += lax.dot_general(qs, f_ref[:, at], LAST, preferred_element_type=F32)
        accmt[...] += lax.dot_general(qs, tar_ref[:, at], LAST, preferred_element_type=F32)
        basket = jnp.sum(share * e, axis=0, keepdims=True)
        arg = (basket - 1.0) * (1.0 / soft_width)
        small = jnp.exp(-jnp.abs(arg))
        plus = jnp.maximum(arg, 0.0) + jnp.log1p(small)
        slope = jnp.where(arg >= 0.0, 1.0, small) / (1.0 + small)
        taken = ex_ref[:, at].astype(F32)
        bar = taken * (notional * slope)
        rew_out[:, at] = taken * (notional * soft_width * plus)
        bar_out[:, at] = bar
        dd = bar * (e - basket)
        vv = bar * drift
        for j in range(width // 128):
            accd[...] += dd[:, j * 128 : (j + 1) * 128]
            accv[...] += vv[:, j * 128 : (j + 1) * 128]
        return carry

    cut = chunks
    lax.fori_loop(0, cut, adjoint_step, 0)

    rest = (accm[: 5 * A, :N] + (accm[: 5 * A, N:] + accm[5 * A :, :N])) + accm[5 * A :, N:]
    for j in range(20):
        pay[GSLOTS + j] = rest[8 * j : 8 * j + 8, :]
    lane8 = lax.broadcasted_iota(jnp.int32, (8, N), 1)
    cols = []
    dsum = jnp.sum(accd[...], axis=1, keepdims=True)
    vsum = jnp.sum(accv[...], axis=1, keepdims=True)
    mt = accmt[: 5 * A, :] + accmt[5 * A :, :]
    mcf = mt[:, 0:1] + mt[:, 1:2] + mt[:, 2:3]
    mfree = mt[:, 3:4]
    for x, count in ((dsum, 4), (vsum, 4), (mcf, 20), (mfree, 20)):
        cols += [x[8 * i : 8 * i + 8, :] for i in range(count)]
    extra = jnp.zeros((8, N), F32)
    for i, x in enumerate(cols):
        extra = jnp.where(lane8 == i, x, extra)
    pay[SLOTS - 1] = extra

    if comm:
        @pl.when(owns_gram)
        def _():
            z_stage()

        rs_start(GSLOTS, SLOTS)

        @pl.when(owns_rest)
        def _():
            z_stage()

        @pl.when(owns_gram)
        def _():
            ag_stage()

        ag_wait(0, GSLOTS)

        @pl.when(owns_rest)
        def _():
            ag_stage()
    else:
        total[...] = pay[...]

    per_path = 1.0 / total_paths
    packed = jnp.concatenate([total[j] for j in range(8)], axis=0)
    upper = jnp.where(lane > prow, packed, jnp.where(lane == prow, 0.5 * packed, 0.0))
    tail = total[8]
    lower = jnp.where(
        lane == prow, 0.5 * jnp.broadcast_to(tail[2:3, :], (N // 2, N)), jnp.where(lane < prow, packed, 0.0)
    )
    lower = pltpu.roll(jnp.where(lane < N // 2, lower, 0.0), N // 2, 1)
    folded = jnp.concatenate([upper, lower], axis=0) * per_path
    gram = folded + folded.T
    sol = solve(gram, jnp.where(r8 < 2, tail, 0.0) * per_path)
    reg, mult = sol[0:1, :], sol[1:2, :]
    big = lax.broadcasted_iota(jnp.int32, (N, N), 0)
    coef = jnp.where(big == 0, reg, jnp.where(big == 1, mult, 0.0)).T
    coef_out[...] = coef

    if comm:
        ag_wait(GSLOTS, SLOTS)
    extra = total[SLOTS - 1]
    vega = [jnp.zeros((8, 1), F32) for _ in range(4)]
    for kind in range(5):
        at = A * (kind if kind < 3 else kind - 1)
        cr, cm = coef[at : at + A, 0:1], coef[at : at + A, 1:2]
        if kind == 3:
            cr = jnp.concatenate([cr[A - 1 :], cr[: A - 1]], axis=0)
            cm = jnp.concatenate([cm[A - 1 :], cm[: A - 1]], axis=0)
        if kind == 1:
            cr, cm = cr * root_two, cm * root_two
        for i in range(4):
            j = 4 * kind + i
            block = total[GSLOTS + j]
            mr = extra[:, 8 + j : 9 + j] - jnp.sum(block * reg, axis=1, keepdims=True)
            mm = extra[:, 28 + j : 29 + j] - jnp.sum(block * mult, axis=1, keepdims=True)
            lo = 8 * i
            vega[i] = vega[i] + cm[lo : lo + 8] * mr + cr[lo : lo + 8] * mm
    delta = weight / whole * jnp.concatenate([extra[:, i : i + 1] for i in range(4)], axis=0)
    vrew = (root_time * share) * jnp.concatenate([extra[:, 4 + i : 5 + i] for i in range(4)], axis=0)
    vega = jnp.concatenate(vega, axis=0) + vrew
    glane = lax.broadcasted_iota(jnp.int32, (A, N), 1)
    both = jnp.where(glane == 0, delta, jnp.where(glane == 1, vega, 0.0)) * per_path
    both = jnp.concatenate([both, jnp.zeros((N - A, N), F32)], axis=0).T
    greek_out[...] = both[0:8, :]

    def finish(c, carry):
        for copy in out_copies(c):
            copy.wait()
        return carry

    lax.fori_loop(0, chunks, finish, 0)
    if comm:
        def sent_slot(slot, carry):
            @pl.when(me != slot)
            def _():
                rs_copy(slot).wait_send()

            return carry

        lax.fori_loop(0, SLOTS, sent_slot, 0)

        @pl.when(me < SLOTS)
        def _():
            def sent_z(d, carry):
                z_copy(d).wait_send()
                return carry

            lax.fori_loop(1, nz, sent_z, 0)

            def sent_ag(d, carry):
                ag_copy(d).wait_send()
                return carry

            lax.fori_loop(1, plane, sent_ag, 0)


def second_kernel(
    s_ref, t_ref, cf_ref, ex_ref, rew_ref, bar_ref, coef_ref, greek_ref, spot_ref, vol_ref, wei_ref,
    value_out, cot_out, flow_out, greeks,
):
    vol = column(vol_ref[...], A)
    spot = column(spot_ref[...], A)
    weight = column(wei_ref[...], A)
    scale = 1.0 / (spot * (vol * root_time))
    share = weight / jnp.sum(weight * spot, axis=0, keepdims=True)
    s, t = s_ref[...], t_ref[...]
    up, down = pltpu.roll(s, A - 1, 0), pltpu.roll(s, 1, 0)
    flat = 1.0 - t * t
    fits, bars = [], []
    for i in range(2):
        c1, c2, c3, c4 = (coef_ref[A * b : A * (b + 1), i : i + 1] for b in range(4))
        c2 = c2 * inv_root_two
        c3d = jnp.concatenate([c3[A - 1 :], c3[: A - 1]], axis=0)
        square = c2 * s
        lead = c1 + square + c3 * up
        fits.append(
            jnp.sum(s * lead + c4 * t, axis=0, keepdims=True) - jnp.sum(c2, axis=0, keepdims=True)
        )
        bars.append(lead + square + c3d * down + c4 * flat)
    taken = ex_ref[...].astype(F32)
    free = 1.0 - taken
    cont, lam = fits
    value_out[...] = rew_ref[...] + free * cont
    flow_out[...] = lam
    cot_out[...] = scale * ((cf_ref[...] - cont) * bars[1] + (free - lam) * bars[0]) + share * bar_ref[...]
    greeks[...] = greek_ref[0:2, 0:A]


def per_device(dims, total_paths, normals, spot, vol, weights, cash_flows, exercise, width=2048, width2=2048):
    local = normals.shape[1]
    chunks = local // width
    spot, vol, weights = (x.reshape(1, A) for x in (spot, vol, weights))
    cash_flows, exercise = cash_flows.reshape(1, local), exercise.reshape(1, local)
    vmem = pl.BlockSpec(memory_space=pltpu.VMEM)
    hbm = pl.BlockSpec(memory_space=pl.ANY)
    comm = dims is not None
    nz, plane = (dims[3], dims[0] * dims[1] * dims[2]) if comm else (2, 2)
    dma = pltpu.SemaphoreType.DMA
    s, t, rew, bar, coef, greek = pl.pallas_call(
        functools.partial(first_kernel, dims, total_paths, width),
        out_shape=(
            jax.ShapeDtypeStruct((A, local), F32), jax.ShapeDtypeStruct((A, local), F32),
            jax.ShapeDtypeStruct((1, local), F32), jax.ShapeDtypeStruct((1, local), F32),
            jax.ShapeDtypeStruct((N, N), F32), jax.ShapeDtypeStruct((8, N), F32),
        ),
        in_specs=[hbm] + [vmem] * 5,
        out_specs=(hbm, hbm, vmem, vmem, vmem, vmem),
        scratch_shapes=[
            pltpu.VMEM((A, local), F32), pltpu.VMEM((A, local), F32), pltpu.VMEM((A, local), F32),
            pltpu.VMEM((2 * N, local), BF16), pltpu.VMEM((16, local), BF16), pltpu.VMEM((10 * A, width), BF16),
            pltpu.VMEM((2 * N, 2 * N), F32), pltpu.VMEM((16, 2 * N), F32),
            pltpu.VMEM((10 * A, 2 * N), F32), pltpu.VMEM((10 * A, 16), F32),
            pltpu.VMEM((A, 128), F32), pltpu.VMEM((A, 128), F32),
            pltpu.VMEM((SLOTS, 8, N), F32), pltpu.VMEM((plane, 8, N), F32),
            pltpu.VMEM((nz, 8, N), F32), pltpu.VMEM((SLOTS, 8, N), F32),
            dma((chunks,)), dma((2, chunks)), dma((SLOTS,)), dma((plane,)),
            dma((nz,)), dma((nz,)), dma((plane,)), dma((SLOTS,)),
        ],
        compiler_params=pltpu.CompilerParams(
            has_side_effects=True, vmem_limit_bytes=48 * 2**20, **({"collective_id": 0} if comm else {})
        ),
        name="normal_equations",
    )(normals, spot, vol, weights, cash_flows, exercise)
    wide = pl.BlockSpec((A, width2), lambda i: (0, i))
    flat = pl.BlockSpec((1, width2), lambda i: (0, i))

    def fixed(*shape):
        return pl.BlockSpec(shape, lambda i: (0, 0))

    value, cot, flow, greeks = pl.pallas_call(
        second_kernel,
        grid=(local // width2,),
        out_shape=(
            jax.ShapeDtypeStruct((1, local), F32), jax.ShapeDtypeStruct((A, local), F32),
            jax.ShapeDtypeStruct((1, local), F32), jax.ShapeDtypeStruct((2, A), F32),
        ),
        in_specs=[wide, wide, flat, flat, flat, flat, fixed(N, N), fixed(8, N)] + [fixed(1, A)] * 3,
        out_specs=(flat, wide, flat, fixed(2, A)),
        compiler_params=pltpu.CompilerParams(vmem_limit_bytes=32 * 2**20),
        name="path_outputs",
    )(s, t, cash_flows, exercise, rew, bar, coef, greek, spot, vol, weights)
    return value.reshape(local), cot, flow.reshape(local), greeks


def solution(mesh):
    shape = dict(mesh.shape)
    ncore, ny = 2, 4
    dims = (shape["grp"] // ncore, ncore, ny, shape["path"] // ny)
    count = shape["grp"] * shape["path"]

    def body(normals, *rest):
        return per_device(dims, normals.shape[1] * count, normals, *rest)

    split_paths = ("grp", "path")
    in_specs = (P(None, split_paths), P(), P(), P(), P(split_paths), P(split_paths))
    out_specs = (P(split_paths), P(None, split_paths), P(split_paths), P())
    return jax.shard_map(body, mesh=mesh, in_specs=in_specs, out_specs=out_specs, check_vma=False)
```

```python
import functools
import math

import jax
import jax.numpy as jnp
from jax import lax
from jax.experimental import pallas as pl
from jax.experimental.pallas import tpu as pltpu
from jax.sharding import PartitionSpec as P

MESH = pl.DeviceIdType.MESH
F32, BF16 = jnp.float32, jnp.bfloat16
expiry_time = 0.5
root_time = math.sqrt(0.5)
inv_root_two = 1.0 / math.sqrt(2.0)
root_two = math.sqrt(2.0)
notional = 20.0
soft_width = 0.02
LAST = (((1,), (1,)), ((), ()))
A = 32
N = 4 * A
GSLOTS = 9
SUB, SUB2 = 256, 256
SLOTS = 30


def column(row, size):
    eye = lax.broadcasted_iota(jnp.int32, (size, size), 0) == lax.broadcasted_iota(
        jnp.int32, (size, size), 1
    )
    return jnp.sum(jnp.where(eye, jnp.broadcast_to(row, (size, size)), 0.0), axis=1, keepdims=True)


def split(x):
    hi = x.astype(BF16)
    return hi, (x - hi.astype(F32)).astype(BF16)


def solve(g, b):
    lane = lax.broadcasted_iota(jnp.int32, (8, N), 1)
    rows = [g[8 * i : 8 * i + 8, :] for i in range(N // 8)] + [b]
    for k in range(0, N, 4):
        tile = rows[k // 8]
        pivot = []
        for q in range(4):
            r = k % 8 + q
            pivot.append(jnp.broadcast_to(tile[r : r + 1, :], (8, N)))

        def at(i, j):
            return jnp.broadcast_to(pivot[i][:, k + j : k + j + 1], (8, N))

        a, h, c = at(0, 0), at(0, 1), at(1, 1)
        b00, b01, b10, b11 = at(0, 2), at(0, 3), at(1, 2), at(1, 3)
        d00, d01, d11 = at(2, 2), at(2, 3), at(3, 3)
        inv = 1.0 / (a * c - h * h)
        i00, i01, i11 = c * inv, -(h * inv), a * inv
        e00, e01 = i00 * b00 + i01 * b10, i00 * b01 + i01 * b11
        e10, e11 = i01 * b00 + i11 * b10, i01 * b01 + i11 * b11
        s00 = d00 - (b00 * e00 + b10 * e10)
        s01 = d01 - (b00 * e01 + b10 * e11)
        s11 = d11 - (b01 * e01 + b11 * e11)
        inv = 1.0 / (s00 * s11 - s01 * s01)
        w00, w01, w11 = s11 * inv, -(s01 * inv), s00 * inv
        r0, r1, r2, r3 = (pivot[q] - (lane == k + q).astype(F32) for q in range(4))
        t2 = r2 - (e00 * r0 + e10 * r1)
        t3 = r3 - (e01 * r0 + e11 * r1)
        low0 = w00 * t2 + w01 * t3
        low1 = w01 * t2 + w11 * t3
        up0 = (i00 * r0 + i01 * r1) - (e00 * low0 + e01 * low1)
        up1 = (i01 * r0 + i11 * r1) - (e10 * low0 + e11 * low1)
        first = k // 8 if k % 8 == 0 else k // 8 + 1
        for i in range(first, N // 8 + 1):
            x = rows[i]
            c0, c1, c2, c3 = (jnp.broadcast_to(x[:, k + q : k + q + 1], (8, N)) for q in range(4))
            rows[i] = x - ((c0 * up0 + c1 * up1) + (c2 * low0 + c3 * low1))
    return rows[N // 8]


def first_kernel(
    dims, total_paths, width,
    z_hbm, spot_hbm, vol_hbm, wei_hbm, cf_hbm, ex_hbm,
    s_ref, t_ref, cf_ref, free_ref, rew_out, bar_out, coef_out, greek_out,
    z_ref, spot_ref, vol_ref, wei_ref, ex_ref, fe_ref, fo_ref, tar_ref, q_ref, const,
    acc, acct, accm, accc, accd, accv,
    pay, recv, zrecv, total,
    in_sem, par_sem, rs_send, rs_recv, z_send, z_recv, ag_send, ag_recv,
):
    local = z_ref.shape[1]
    chunks = local // width
    comm = dims is not None
    if comm:
        nx, ncore, ny, nz = dims
        plane = nx * ncore * ny
        grp, path = lax.axis_index("grp"), lax.axis_index("path")
        my_z, my_y = path // ny, path % ny
        my_x, my_core = grp // ncore, grp % ncore
        me = (my_core * ny + my_y) * nx + my_x

        def place(slot, z):
            x, y, core = slot % nx, (slot // nx) % ny, slot // (nx * ny)
            return (x * ncore + core, z * ny + y)

        barrier = pltpu.get_barrier_semaphore()

        def greet_z(d, carry):
            peer = place(me, (my_z + d) % nz)
            pl.semaphore_signal(barrier, inc=1, device_id=peer, device_id_type=MESH)
            return carry

        def greet_plane(d, carry):
            peer = place((me + d) % plane, my_z)
            pl.semaphore_signal(barrier, inc=1, device_id=peer, device_id_type=MESH)
            return carry

        lax.fori_loop(1, nz, greet_z, 0)
        lax.fori_loop(1, plane, greet_plane, 0)

    def in_copy(c):
        at = pl.ds(pl.multiple_of(c * width, width), width)
        return pltpu.make_async_copy(z_hbm.at[:, at], z_ref.at[:, at], in_sem.at[c])

    small = [
        pltpu.make_async_copy(src, dst, par_sem.at[i])
        for i, (src, dst) in enumerate(
            ((spot_hbm, spot_ref), (vol_hbm, vol_ref), (wei_hbm, wei_ref), (cf_hbm, cf_ref), (ex_hbm, ex_ref))
        )
    ]
    for i in (1, 0, 2):
        small[i].start()
    in_copy(0).start()
    small[3].start()
    small[4].start()
    for c in range(1, chunks):
        in_copy(c).start()
    for i in range(3):
        small[i].wait()

    vol = column(vol_ref[...], A)
    spot = column(spot_ref[...], A)
    weight = column(wei_ref[...], A)
    spread = vol * root_time
    whole = jnp.sum(weight * spot, axis=0, keepdims=True)
    share = weight * spot / whole
    for i, x in enumerate(
        (spread, 0.5 * expiry_time * (vol * vol), 1.0 / spread, 1.0 / vol, share)
    ):
        const[i] = jnp.broadcast_to(x, (A, 128))

    def wide(i):
        x = const[i]
        return jnp.concatenate([x] * (SUB // 128), axis=1)

    row = lax.broadcasted_iota(jnp.int32, (A, SUB), 0)
    trow = lax.broadcasted_iota(jnp.int32, (16, SUB), 0)

    acc[...] = jnp.zeros_like(acc)
    acct[...] = jnp.zeros_like(acct)
    small[3].wait()
    small[4].wait()

    def basis(c, f_ref, half):
        in_copy(c).wait()
        for b in range(width // SUB):
            at = pl.ds(pl.multiple_of(c * width + b * SUB, SUB), SUB)
            to = pl.ds(pl.multiple_of(half * width + b * SUB, SUB), SUB)
            e = jnp.exp(wide(0) * z_ref[:, at] - wide(1))
            s = (e - 1.0) * wide(2)
            t = jnp.where(row == A - 1, 1.0, jnp.tanh(s))
            s_ref[:, at] = s
            t_ref[:, at] = t
            free = 1.0 - ex_ref[:, at].astype(F32)
            free_ref[:, at] = free
            blocks = (s, (s * s - 1.0) * inv_root_two, s * pltpu.roll(s, A - 1, 0), t)
            for i, x in enumerate(blocks):
                hi, lo = split(x)
                if i == 3:
                    lo = (x - hi.astype(F32))
                    lo = jnp.where(row == A - 1, jnp.broadcast_to(free, (A, SUB)), lo).astype(BF16)
                f_ref[i * A : (i + 1) * A, to] = hi
                f_ref[N + i * A : N + (i + 1) * A, to] = lo
            cf = jnp.broadcast_to(cf_ref[:, at], (16, SUB))
            c0 = cf.astype(BF16).astype(F32)
            c1 = (cf - c0).astype(BF16).astype(F32)
            c2 = cf - c0 - c1
            tar_ref[:, at] = jnp.where(
                trow == 0, c0, jnp.where(trow == 1, c1, jnp.where(trow == 2, c2, 0.0))
            ).astype(BF16)

    def gram_dot(c, f_ref, half):
        f = f_ref[:, pl.ds(pl.multiple_of(half * width, width), width)]
        acc[...] += lax.dot_general(f, f, LAST, preferred_element_type=F32)
        at = pl.ds(pl.multiple_of(c * width, width), width)
        acct[...] += lax.dot_general(tar_ref[:, at], f, LAST, preferred_element_type=F32)

    pairs = chunks // 2
    basis(0, fe_ref, 0)

    def gram_step(i, carry):
        basis(2 * i + 1, fo_ref, i)
        gram_dot(2 * i, fe_ref, i)
        basis(2 * i + 2, fe_ref, i + 1)
        gram_dot(2 * i + 1, fo_ref, i)
        return carry

    lax.fori_loop(0, pairs - 1, gram_step, 0)
    basis(chunks - 1, fo_ref, pairs - 1)
    gram_dot(chunks - 2, fe_ref, pairs - 1)
    gram_dot(chunks - 1, fo_ref, pairs - 1)

    low_row = lax.broadcasted_iota(jnp.int32, (N, N), 0) < N - 1
    low_col = lax.broadcasted_iota(jnp.int32, (N, N), 1) < N - 1
    cross = jnp.where(low_col, acc[:N, N:], 0.0) + jnp.where(low_row, acc[N:, :N], 0.0)
    gram = (acc[:N, :N] + cross) + jnp.where(jnp.logical_and(low_row, low_col), acc[N:, N:], 0.0)
    lane1 = lax.broadcasted_iota(jnp.int32, (16, N), 1)
    moment = acct[:, :N] + jnp.where(lane1 < N - 1, acct[:, N:], 0.0)
    lane1 = lax.broadcasted_iota(jnp.int32, (1, N), 1)
    moment_free = acc[2 * N - 1 :, :N] + jnp.where(lane1 < N - 1, acc[2 * N - 1 :, N:], 0.0)
    lane = lax.broadcasted_iota(jnp.int32, (N // 2, N), 1)
    prow = lax.broadcasted_iota(jnp.int32, (N // 2, N), 0)
    corner = pltpu.roll(gram[N // 2 :, :], N // 2, 1)
    packed = jnp.where(lane < prow, corner, gram[: N // 2, :])
    diagonal = jnp.sum(jnp.where(lane == prow, corner, 0.0), axis=0, keepdims=True)
    for j in range(8):
        pay[j] = packed[8 * j : 8 * j + 8, :]
    r8 = lax.broadcasted_iota(jnp.int32, (8, N), 0)
    pay[8] = jnp.where(
        r8 == 0,
        moment[0:1, :] + moment[1:2, :] + moment[2:3, :],
        jnp.where(r8 == 1, moment_free, jnp.where(r8 == 2, diagonal, 0.0)),
    )

    def rs_copy(slot):
        return pltpu.make_async_remote_copy(
            src_ref=pay.at[slot], dst_ref=recv.at[me], send_sem=rs_send.at[slot], recv_sem=rs_recv.at[me],
            device_id=place(slot, my_z), device_id_type=MESH,
        )

    def rs_start(low, high):
        for slot in range(low, high):
            @pl.when(me != slot)
            def _():
                rs_copy(slot).start()

            @pl.when(me == slot)
            def _():
                recv[me] = pay[slot]

    def arrived(buffer, sem, i):
        return pltpu.make_async_remote_copy(
            src_ref=buffer.at[i], dst_ref=buffer.at[i], send_sem=rs_send.at[0], recv_sem=sem.at[i],
            device_id=place(me, my_z), device_id_type=MESH,
        )

    def z_copy(d):
        return pltpu.make_async_remote_copy(
            src_ref=zrecv.at[my_z], dst_ref=zrecv.at[my_z], send_sem=z_send.at[d], recv_sem=z_recv.at[my_z],
            device_id=place(me, (my_z + d) % nz), device_id_type=MESH,
        )

    def ag_copy(d):
        return pltpu.make_async_remote_copy(
            src_ref=total.at[me], dst_ref=total.at[me], send_sem=ag_send.at[d], recv_sem=ag_recv.at[me],
            device_id=place((me + d) % plane, my_z), device_id_type=MESH,
        )

    def z_stage():
        def wait(d, carry):
            arrived(recv, rs_recv, (me + d) % plane).wait_recv()
            return carry

        lax.fori_loop(1, plane, wait, 0)
        parts = [recv[i] for i in range(plane)]
        while len(parts) > 1:
            parts = [parts[i] + parts[i + 1] for i in range(0, len(parts), 2)]
        zrecv[my_z] = parts[0]
        for i in range(nz // 2):
            for d in ((nz // 2,) if i == 0 else (nz // 2 - i, nz // 2 + i)):
                z_copy(d).start()

    def ag_stage():
        def wait(d, carry):
            arrived(zrecv, z_recv, (my_z + d) % nz).wait_recv()
            return carry

        lax.fori_loop(1, nz, wait, 0)
        parts = [zrecv[i] for i in range(nz)]
        while len(parts) > 1:
            parts = [parts[i] + parts[i + 1] for i in range(0, len(parts), 2)]
        total[me] = parts[0]

        def send(d, carry):
            ag_copy(d).start()
            return carry

        lax.fori_loop(1, plane, send, 0)

    def ag_wait(low, high):
        def wait(slot, carry):
            @pl.when(me != slot)
            def _():
                arrived(total, ag_recv, slot).wait_recv()

            return carry

        lax.fori_loop(low, high, wait, 0)

    owns_gram = owns_rest = None
    if comm:
        owns_gram = me < GSLOTS
        owns_rest = jnp.logical_and(me >= GSLOTS, me < SLOTS)
        pl.semaphore_wait(barrier, nz - 1 + plane - 1)
        rs_start(0, GSLOTS)

    accm[...] = jnp.zeros_like(accm)
    accc[...] = jnp.zeros_like(accc)
    accd[...] = jnp.zeros_like(accd)
    accv[...] = jnp.zeros_like(accv)

    def adjoint(c, slot):
        sums = [jnp.zeros((A, SUB), F32) for _ in range(7)]
        for b in range(width // SUB):
            at = pl.ds(pl.multiple_of(c * width + b * SUB, SUB), SUB)
            to = pl.ds(b * SUB, SUB)
            s, t = s_ref[:, at], t_ref[:, at]
            spread = wide(0)
            e = 1.0 + s * spread
            drift = e * (z_ref[:, at] - spread)
            q = (drift - s) * wide(3)
            cf = cf_ref[:, at]
            for i, x in enumerate(
                (q, q * s, q * pltpu.roll(s, A - 1, 0), q * pltpu.roll(s, 1, 0), q * (1.0 - t * t))
            ):
                hi, lo = split(x)
                q_ref[slot, i * A : (i + 1) * A, to] = hi
                q_ref[slot, (5 + i) * A : (6 + i) * A, to] = lo
                sums[i] = sums[i] + x * cf
            basket = jnp.sum(wide(4) * e, axis=0, keepdims=True)
            arg = (basket - 1.0) * (1.0 / soft_width)
            tiny = jnp.exp(-jnp.abs(arg))
            plus = jnp.maximum(arg, 0.0) + jnp.log1p(tiny)
            slope = jnp.where(arg >= 0.0, 1.0, tiny) / (1.0 + tiny)
            taken = 1.0 - free_ref[:, at]
            bar = taken * (notional * slope)
            rew_out[:, at] = taken * (notional * soft_width * plus)
            bar_out[:, at] = bar
            sums[5] = sums[5] + bar * (e - basket)
            sums[6] = sums[6] + bar * drift
        for i, x in enumerate(sums):
            folded = x[:, :128]
            for j in range(1, SUB // 128):
                folded = folded + x[:, j * 128 : (j + 1) * 128]
            if i < 5:
                accc[i * A : (i + 1) * A, :] += folded
            else:
                (accd, accv)[i - 5][...] += folded

    def rest_dot(slot, f_ref, half):
        f = f_ref[:, pl.ds(pl.multiple_of(half * width, width), width)]
        accm[...] += lax.dot_general(q_ref[slot], f, LAST, preferred_element_type=F32)

    def adjoint_step(i, carry):
        adjoint(2 * i + 1, 1)
        rest_dot(0, fe_ref, i)
        adjoint(2 * i + 2, 0)
        rest_dot(1, fo_ref, i)
        return carry

    adjoint(0, 0)
    cut = pairs - 1
    lax.fori_loop(0, cut, adjoint_step, 0)
    if comm:
        @pl.when(owns_gram)
        def _():
            z_stage()

    adjoint(chunks - 1, 1)
    rest_dot(0, fe_ref, pairs - 1)
    rest_dot(1, fo_ref, pairs - 1)

    lowl = lax.broadcasted_iota(jnp.int32, (5 * A, N), 1) < N - 1
    right = accm[: 5 * A, N:] + accm[5 * A :, N:]
    rest = (accm[: 5 * A, :N] + accm[5 * A :, :N]) + jnp.where(lowl, right, 0.0)
    mfree = right[:, N - 1 : N]
    for j in range(20):
        pay[GSLOTS + j] = rest[8 * j : 8 * j + 8, :]
    lane8 = lax.broadcasted_iota(jnp.int32, (8, N), 1)
    cols = []
    dsum = jnp.sum(accd[...], axis=1, keepdims=True)
    vsum = jnp.sum(accv[...], axis=1, keepdims=True)
    mcf = jnp.sum(accc[...], axis=1, keepdims=True)
    for x, count in ((dsum, 4), (vsum, 4), (mcf, 20), (mfree, 20)):
        cols += [x[8 * i : 8 * i + 8, :] for i in range(count)]
    extra = jnp.zeros((8, N), F32)
    for i, x in enumerate(cols):
        extra = jnp.where(lane8 == i, x, extra)
    pay[SLOTS - 1] = extra

    if comm:
        rs_start(GSLOTS, SLOTS)

        @pl.when(owns_rest)
        def _():
            z_stage()

        @pl.when(owns_gram)
        def _():
            ag_stage()

        ag_wait(0, GSLOTS)

        @pl.when(owns_rest)
        def _():
            ag_stage()
    else:
        total[...] = pay[...]

    per_path = 1.0 / total_paths
    packed = jnp.concatenate([total[j] for j in range(8)], axis=0)
    upper = jnp.where(lane > prow, packed, jnp.where(lane == prow, 0.5 * packed, 0.0))
    tail = total[8]
    lower = jnp.where(
        lane == prow, 0.5 * jnp.broadcast_to(tail[2:3, :], (N // 2, N)), jnp.where(lane < prow, packed, 0.0)
    )
    lower = pltpu.roll(jnp.where(lane < N // 2, lower, 0.0), N // 2, 1)
    folded = jnp.concatenate([upper, lower], axis=0) * per_path
    gram = folded + folded.T
    sol = solve(gram, jnp.where(r8 < 2, tail, 0.0) * per_path)
    reg, mult = sol[0:1, :], sol[1:2, :]
    big = lax.broadcasted_iota(jnp.int32, (N, N), 0)
    coef = jnp.where(big == 0, reg, jnp.where(big == 1, mult, 0.0)).T
    coef_out[...] = coef

    if comm:
        ag_wait(GSLOTS, SLOTS)
    extra = total[SLOTS - 1]
    vega = [jnp.zeros((8, 1), F32) for _ in range(4)]
    for kind in range(5):
        at = A * (kind if kind < 3 else kind - 1)
        cr, cm = coef[at : at + A, 0:1], coef[at : at + A, 1:2]
        if kind == 3:
            cr = jnp.concatenate([cr[A - 1 :], cr[: A - 1]], axis=0)
            cm = jnp.concatenate([cm[A - 1 :], cm[: A - 1]], axis=0)
        if kind == 1:
            cr, cm = cr * root_two, cm * root_two
        for i in range(4):
            j = 4 * kind + i
            block = total[GSLOTS + j]
            mr = extra[:, 8 + j : 9 + j] - jnp.sum(block * reg, axis=1, keepdims=True)
            mm = extra[:, 28 + j : 29 + j] - jnp.sum(block * mult, axis=1, keepdims=True)
            lo = 8 * i
            vega[i] = vega[i] + cm[lo : lo + 8] * mr + cr[lo : lo + 8] * mm
    delta = weight / whole * jnp.concatenate([extra[:, i : i + 1] for i in range(4)], axis=0)
    vrew = (root_time * share) * jnp.concatenate([extra[:, 4 + i : 5 + i] for i in range(4)], axis=0)
    vega = jnp.concatenate(vega, axis=0) + vrew
    glane = lax.broadcasted_iota(jnp.int32, (A, N), 1)
    both = jnp.where(glane == 0, delta, jnp.where(glane == 1, vega, 0.0)) * per_path
    both = jnp.concatenate([both, jnp.zeros((N - A, N), F32)], axis=0).T
    greek_out[...] = both[0:8, :]

    if comm:
        def sent_slot(slot, carry):
            @pl.when(me != slot)
            def _():
                rs_copy(slot).wait_send()

            return carry

        lax.fori_loop(0, SLOTS, sent_slot, 0)

        @pl.when(me < SLOTS)
        def _():
            def sent_z(d, carry):
                z_copy(d).wait_send()
                return carry

            lax.fori_loop(1, nz, sent_z, 0)

            def sent_ag(d, carry):
                ag_copy(d).wait_send()
                return carry

            lax.fori_loop(1, plane, sent_ag, 0)


def second_kernel(
    width, s_ref, t_ref, cf_ref, free_ref, rew_ref, bar_ref, coef_ref, greek_ref, spot_hbm, vol_hbm, wei_hbm,
    value_hbm, cot_hbm, flow_hbm, greek_hbm,
    spot_ref, vol_ref, wei_ref, const, value_ref, cot_ref, flow_ref, greeks, par_sem, out_sem,
):
    local = s_ref.shape[1]
    chunks = local // width
    small = [
        pltpu.make_async_copy(src, dst, par_sem.at[i])
        for i, (src, dst) in enumerate(((spot_hbm, spot_ref), (vol_hbm, vol_ref), (wei_hbm, wei_ref)))
    ]
    for copy in small:
        copy.start()

    def outs(c):
        at = pl.ds(pl.multiple_of(c * width, width), width)
        return [
            pltpu.make_async_copy(src.at[:, at], dst.at[:, at], out_sem.at[i, c])
            for i, (src, dst) in enumerate(((cot_ref, cot_hbm), (value_ref, value_hbm), (flow_ref, flow_hbm)))
        ]

    offsets = []
    for i in range(2):
        c1, c2, c3, c4 = (coef_ref[A * b : A * (b + 1), i : i + 1] for b in range(4))
        c2 = c2 * inv_root_two
        c3d = jnp.concatenate([c3[A - 1 :], c3[: A - 1]], axis=0)
        for j, x in enumerate((c1, c2, c3, c3d, c4)):
            const[5 * i + j] = jnp.broadcast_to(x, (A, 128))
        offsets.append(jnp.sum(c2, axis=0, keepdims=True))
    greeks[...] = greek_ref[0:2, 0:A]
    last = pltpu.make_async_copy(greeks, greek_hbm, par_sem.at[3])
    last.start()
    for copy in small:
        copy.wait()
    vol = column(vol_ref[...], A)
    spot = column(spot_ref[...], A)
    weight = column(wei_ref[...], A)
    scale = 1.0 / (spot * (vol * root_time))
    share = weight / jnp.sum(weight * spot, axis=0, keepdims=True)
    const[10] = jnp.broadcast_to(scale, (A, 128))
    const[11] = jnp.broadcast_to(share, (A, 128))

    def wide(i):
        x = const[i]
        return jnp.concatenate([x] * (SUB2 // 128), axis=1)

    def step(c, carry):
        for b in range(width // SUB2):
            at = pl.ds(pl.multiple_of(c * width + b * SUB2, SUB2), SUB2)
            s, t = s_ref[:, at], t_ref[:, at]
            up, down = pltpu.roll(s, A - 1, 0), pltpu.roll(s, 1, 0)
            flat = 1.0 - t * t
            fits, bars = [], []
            for i in range(2):
                square = wide(5 * i + 1) * s
                lead = wide(5 * i) + square + wide(5 * i + 2) * up
                c4 = wide(5 * i + 4)
                fits.append(jnp.sum(s * lead + c4 * t, axis=0, keepdims=True) - offsets[i])
                bars.append(lead + square + wide(5 * i + 3) * down + c4 * flat)
            free = free_ref[:, at]
            cont, lam = fits
            value_ref[:, at] = rew_ref[:, at] + free * cont
            flow_ref[:, at] = lam
            cot_ref[:, at] = (
                wide(10) * ((cf_ref[:, at] - cont) * bars[1] + (free - lam) * bars[0]) + wide(11) * bar_ref[:, at]
            )
        for copy in outs(c):
            copy.start()
        return carry

    lax.fori_loop(0, chunks, step, 0)

    def finish(c, carry):
        for copy in outs(c):
            copy.wait()
        return carry

    lax.fori_loop(0, chunks, finish, 0)
    last.wait()


def per_device(dims, total_paths, normals, spot, vol, weights, cash_flows, exercise, width=2048, width2=2048):
    comm = dims is not None
    local = normals.shape[1]
    chunks = local // width
    spot, vol, weights = (x.reshape(1, A) for x in (spot, vol, weights))
    cash_flows, exercise = cash_flows.reshape(1, local), exercise.reshape(1, local)
    if comm:
        normals, spot, vol, weights, cash_flows, exercise = (
            pltpu.with_memory_space_constraint(x, pltpu.HBM)
            for x in (normals, spot, vol, weights, cash_flows, exercise)
        )
    vmem = pl.BlockSpec(memory_space=pltpu.VMEM)
    hbm = pl.BlockSpec(memory_space=pltpu.HBM)
    nz, plane = (dims[3], dims[0] * dims[1] * dims[2]) if comm else (2, 2)
    dma = pltpu.SemaphoreType.DMA
    wide, flat = jax.ShapeDtypeStruct((A, local), F32), jax.ShapeDtypeStruct((1, local), F32)
    half = pltpu.VMEM((2 * N, local // 2), BF16)
    tiny = pltpu.VMEM((1, A), F32)
    *arrays, coef, greek = pl.pallas_call(
        functools.partial(first_kernel, dims, total_paths, width),
        out_shape=(
            wide, wide, flat, flat, flat, flat,
            jax.ShapeDtypeStruct((N, N), F32), jax.ShapeDtypeStruct((8, N), F32),
        ),
        in_specs=[hbm] * 6,
        out_specs=(vmem,) * 8,
        scratch_shapes=[
            pltpu.VMEM((A, local), F32), tiny, tiny, tiny, pltpu.VMEM((1, local), jnp.int32),
            half, half, pltpu.VMEM((16, local), BF16), pltpu.VMEM((2, 10 * A, width), BF16),
            pltpu.VMEM((5, A, 128), F32),
            pltpu.VMEM((2 * N, 2 * N), F32), pltpu.VMEM((16, 2 * N), F32),
            pltpu.VMEM((10 * A, 2 * N), F32), pltpu.VMEM((5 * A, 128), F32),
            pltpu.VMEM((A, 128), F32), pltpu.VMEM((A, 128), F32),
            pltpu.VMEM((SLOTS, 8, N), F32), pltpu.VMEM((plane, 8, N), F32),
            pltpu.VMEM((nz, 8, N), F32), pltpu.VMEM((SLOTS, 8, N), F32),
            dma((chunks,)), dma((5,)), dma((SLOTS,)), dma((plane,)),
            dma((nz,)), dma((nz,)), dma((plane,)), dma((SLOTS,)),
        ],
        compiler_params=pltpu.CompilerParams(
            has_side_effects=True, vmem_limit_bytes=40 * 2**20, **({"collective_id": 0} if comm else {})
        ),
        name="normal_equations",
    )(normals, spot, vol, weights, cash_flows, exercise)
    value, cot, flow, greeks = pl.pallas_call(
        functools.partial(second_kernel, width2),
        out_shape=(flat, wide, flat, jax.ShapeDtypeStruct((2, A), F32)),
        in_specs=[vmem] * 8 + [hbm] * 3,
        out_specs=(hbm,) * 4,
        scratch_shapes=[
            tiny, tiny, tiny, pltpu.VMEM((12, A, 128), F32),
            pltpu.VMEM((1, local), F32), pltpu.VMEM((A, local), F32), pltpu.VMEM((1, local), F32),
            pltpu.VMEM((2, A), F32), dma((4,)), dma((3, local // width2)),
        ],
        compiler_params=pltpu.CompilerParams(vmem_limit_bytes=32 * 2**20),
        name="path_outputs",
    )(*arrays, coef, greek, spot, vol, weights)
    return value.reshape(local), cot, flow.reshape(local), greeks


def solution(mesh):
    shape = dict(mesh.shape)
    ncore, ny = 2, 4
    dims = (shape["grp"] // ncore, ncore, ny, shape["path"] // ny)
    count = shape["grp"] * shape["path"]

    def body(normals, *rest):
        return per_device(dims, normals.shape[1] * count, normals, *rest)

    split_paths = ("grp", "path")
    in_specs = (P(None, split_paths), P(), P(), P(), P(split_paths), P(split_paths))
    out_specs = (P(split_paths), P(None, split_paths), P(split_paths), P())
    return jax.shard_map(body, mesh=mesh, in_specs=in_specs, out_specs=out_specs, check_vma=False)
```

```python
import functools
import math

import jax
import jax.numpy as jnp
from jax import lax
from jax.experimental import pallas as pl
from jax.experimental.pallas import tpu as pltpu
from jax.sharding import PartitionSpec as P

MESH = pl.DeviceIdType.MESH
F32, BF16 = jnp.float32, jnp.bfloat16
expiry_time = 0.5
root_time = math.sqrt(0.5)
inv_root_two = 1.0 / math.sqrt(2.0)
root_two = math.sqrt(2.0)
notional = 20.0
soft_width = 0.02
LAST = (((1,), (1,)), ((), ()))
A = 32
N = 4 * A
GSLOTS = 9
SUB = 256
SLOTS = 30


def column(row, size):
    eye = lax.broadcasted_iota(jnp.int32, (size, size), 0) == lax.broadcasted_iota(
        jnp.int32, (size, size), 1
    )
    return jnp.sum(jnp.where(eye, jnp.broadcast_to(row, (size, size)), 0.0), axis=1, keepdims=True)


def split(x):
    hi = x.astype(BF16)
    return hi, (x - hi.astype(F32)).astype(BF16)


def solve(g, b, between):
    lane = lax.broadcasted_iota(jnp.int32, (8, N), 1)
    rows = [g[8 * i : 8 * i + 8, :] for i in range(N // 8)] + [b]
    for k in range(0, N, 4):
        if k == N // 2:
            between()
        tile = rows[k // 8]
        pivot = []
        for q in range(4):
            r = k % 8 + q
            pivot.append(jnp.broadcast_to(tile[r : r + 1, :], (8, N)))

        def at(i, j):
            return jnp.broadcast_to(pivot[i][:, k + j : k + j + 1], (8, N))

        a, h, c = at(0, 0), at(0, 1), at(1, 1)
        b00, b01, b10, b11 = at(0, 2), at(0, 3), at(1, 2), at(1, 3)
        d00, d01, d11 = at(2, 2), at(2, 3), at(3, 3)
        inv = 1.0 / (a * c - h * h)
        i00, i01, i11 = c * inv, -(h * inv), a * inv
        e00, e01 = i00 * b00 + i01 * b10, i00 * b01 + i01 * b11
        e10, e11 = i01 * b00 + i11 * b10, i01 * b01 + i11 * b11
        s00 = d00 - (b00 * e00 + b10 * e10)
        s01 = d01 - (b00 * e01 + b10 * e11)
        s11 = d11 - (b01 * e01 + b11 * e11)
        inv = 1.0 / (s00 * s11 - s01 * s01)
        w00, w01, w11 = s11 * inv, -(s01 * inv), s00 * inv
        r0, r1, r2, r3 = (pivot[q] - (lane == k + q).astype(F32) for q in range(4))
        t2 = r2 - (e00 * r0 + e10 * r1)
        t3 = r3 - (e01 * r0 + e11 * r1)
        low0 = w00 * t2 + w01 * t3
        low1 = w01 * t2 + w11 * t3
        up0 = (i00 * r0 + i01 * r1) - (e00 * low0 + e01 * low1)
        up1 = (i01 * r0 + i11 * r1) - (e10 * low0 + e11 * low1)
        first = k // 8 if k % 8 == 0 else k // 8 + 1
        for i in range(first, N // 8 + 1):
            x = rows[i]
            c0, c1, c2, c3 = (jnp.broadcast_to(x[:, k + q : k + q + 1], (8, N)) for q in range(4))
            rows[i] = x - ((c0 * up0 + c1 * up1) + (c2 * low0 + c3 * low1))
    return rows[N // 8]


def first_kernel(
    dims, total_paths, width,
    z_hbm, spot_hbm, vol_hbm, wei_hbm, cf_hbm, ex_hbm,
    value_ref, cot_ref, flow_ref, greek_out,
    s_ref, t_ref, up_ref, down_ref, flat_ref, cf_ref, free_ref, rew_ref, bar_ref, z_ref, spot_ref, vol_ref, wei_ref, ex_ref, fe_ref, fo_ref, tar_ref, q_ref, const,
    acc, acct, accm, accc, accd, accv,
    pay, recv, zrecv, total,
    in_sem, par_sem, rs_send, rs_recv, z_send, z_recv, ag_send, ag_recv,
):
    local = z_ref.shape[1]
    chunks = local // width
    comm = dims is not None
    if comm:
        nx, ncore, ny, nz = dims
        plane = nx * ncore * ny
        grp, path = lax.axis_index("grp"), lax.axis_index("path")
        my_z, my_y = path // ny, path % ny
        my_x, my_core = grp // ncore, grp % ncore
        me = (my_core * ny + my_y) * nx + my_x

        def place(slot, z):
            x, y, core = slot % nx, (slot // nx) % ny, slot // (nx * ny)
            return (x * ncore + core, z * ny + y)

        barrier = pltpu.get_barrier_semaphore()

        def greet_z(d, carry):
            peer = place(me, (my_z + d) % nz)
            pl.semaphore_signal(barrier, inc=1, device_id=peer, device_id_type=MESH)
            return carry

        def greet_plane(d, carry):
            peer = place((me + d) % plane, my_z)
            pl.semaphore_signal(barrier, inc=1, device_id=peer, device_id_type=MESH)
            return carry

        lax.fori_loop(1, nz, greet_z, 0)
        lax.fori_loop(1, plane, greet_plane, 0)

    def in_copy(c):
        at = pl.ds(pl.multiple_of(c * width, width), width)
        return pltpu.make_async_copy(z_hbm.at[:, at], z_ref.at[:, at], in_sem.at[c])

    small = [
        pltpu.make_async_copy(src, dst, par_sem.at[i])
        for i, (src, dst) in enumerate(
            ((spot_hbm, spot_ref), (vol_hbm, vol_ref), (wei_hbm, wei_ref), (cf_hbm, cf_ref), (ex_hbm, ex_ref))
        )
    ]
    for i in (1, 0, 2):
        small[i].start()
    in_copy(0).start()
    small[3].start()
    small[4].start()
    for c in range(1, chunks):
        in_copy(c).start()
    for i in range(3):
        small[i].wait()

    vol = column(vol_ref[...], A)
    spot = column(spot_ref[...], A)
    weight = column(wei_ref[...], A)
    spread = vol * root_time
    whole = jnp.sum(weight * spot, axis=0, keepdims=True)
    share = weight * spot / whole
    for i, x in enumerate(
        (spread, 0.5 * expiry_time * (vol * vol), 1.0 / spread, 1.0 / vol, share, 1.0 / (spot * spread), weight / whole)
    ):
        const[i] = jnp.broadcast_to(x, (A, 128))

    def wide(i):
        x = const[i]
        return jnp.concatenate([x] * (SUB // 128), axis=1)

    row = lax.broadcasted_iota(jnp.int32, (A, SUB), 0)
    trow = lax.broadcasted_iota(jnp.int32, (16, SUB), 0)

    acc[...] = jnp.zeros_like(acc)
    acct[...] = jnp.zeros_like(acct)
    small[3].wait()
    small[4].wait()

    def basis(c, f_ref, half):
        in_copy(c).wait()
        for b in range(width // SUB):
            at = pl.ds(pl.multiple_of(c * width + b * SUB, SUB), SUB)
            to = pl.ds(pl.multiple_of(half * width + b * SUB, SUB), SUB)
            e = jnp.exp(wide(0) * z_ref[:, at] - wide(1))
            s = (e - 1.0) * wide(2)
            t = jnp.where(row == A - 1, 1.0, jnp.tanh(s))
            s_ref[:, at] = s
            t_ref[:, at] = t
            free = 1.0 - ex_ref[:, at].astype(F32)
            free_ref[:, at] = free
            blocks = (s, (s * s - 1.0) * inv_root_two, s * pltpu.roll(s, A - 1, 0), t)
            for i, x in enumerate(blocks):
                hi, lo = split(x)
                if i == 3:
                    lo = (x - hi.astype(F32))
                    lo = jnp.where(row == A - 1, jnp.broadcast_to(free, (A, SUB)), lo).astype(BF16)
                f_ref[i * A : (i + 1) * A, to] = hi
                f_ref[N + i * A : N + (i + 1) * A, to] = lo
            cf = jnp.broadcast_to(cf_ref[:, at], (16, SUB))
            c0 = cf.astype(BF16).astype(F32)
            c1 = (cf - c0).astype(BF16).astype(F32)
            c2 = cf - c0 - c1
            tar_ref[:, at] = jnp.where(
                trow == 0, c0, jnp.where(trow == 1, c1, jnp.where(trow == 2, c2, 0.0))
            ).astype(BF16)

    def gram_dot(c, f_ref, half):
        f = f_ref[:, pl.ds(pl.multiple_of(half * width, width), width)]
        acc[...] += lax.dot_general(f, f, LAST, preferred_element_type=F32)
        at = pl.ds(pl.multiple_of(c * width, width), width)
        acct[...] += lax.dot_general(tar_ref[:, at], f, LAST, preferred_element_type=F32)

    pairs = chunks // 2
    basis(0, fe_ref, 0)

    def gram_step(i, carry):
        basis(2 * i + 1, fo_ref, i)
        gram_dot(2 * i, fe_ref, i)
        basis(2 * i + 2, fe_ref, i + 1)
        gram_dot(2 * i + 1, fo_ref, i)
        return carry

    lax.fori_loop(0, pairs - 1, gram_step, 0)
    basis(chunks - 1, fo_ref, pairs - 1)
    gram_dot(chunks - 2, fe_ref, pairs - 1)
    gram_dot(chunks - 1, fo_ref, pairs - 1)

    low_row = lax.broadcasted_iota(jnp.int32, (N, N), 0) < N - 1
    low_col = lax.broadcasted_iota(jnp.int32, (N, N), 1) < N - 1
    cross = jnp.where(low_col, acc[:N, N:], 0.0) + jnp.where(low_row, acc[N:, :N], 0.0)
    gram = (acc[:N, :N] + cross) + jnp.where(jnp.logical_and(low_row, low_col), acc[N:, N:], 0.0)
    lane1 = lax.broadcasted_iota(jnp.int32, (16, N), 1)
    moment = acct[:, :N] + jnp.where(lane1 < N - 1, acct[:, N:], 0.0)
    lane1 = lax.broadcasted_iota(jnp.int32, (1, N), 1)
    moment_free = acc[2 * N - 1 :, :N] + jnp.where(lane1 < N - 1, acc[2 * N - 1 :, N:], 0.0)
    lane = lax.broadcasted_iota(jnp.int32, (N // 2, N), 1)
    prow = lax.broadcasted_iota(jnp.int32, (N // 2, N), 0)
    corner = pltpu.roll(gram[N // 2 :, :], N // 2, 1)
    packed = jnp.where(lane < prow, corner, gram[: N // 2, :])
    diagonal = jnp.sum(jnp.where(lane == prow, corner, 0.0), axis=0, keepdims=True)
    for j in range(8):
        pay[j] = packed[8 * j : 8 * j + 8, :]
    r8 = lax.broadcasted_iota(jnp.int32, (8, N), 0)
    pay[8] = jnp.where(
        r8 == 0,
        moment[0:1, :] + moment[1:2, :] + moment[2:3, :],
        jnp.where(r8 == 1, moment_free, jnp.where(r8 == 2, diagonal, 0.0)),
    )

    def rs_copy(slot):
        return pltpu.make_async_remote_copy(
            src_ref=pay.at[slot], dst_ref=recv.at[me], send_sem=rs_send.at[slot], recv_sem=rs_recv.at[me],
            device_id=place(slot, my_z), device_id_type=MESH,
        )

    def rs_start(low, high):
        for slot in range(low, high):
            @pl.when(me != slot)
            def _():
                rs_copy(slot).start()

            @pl.when(me == slot)
            def _():
                recv[me] = pay[slot]

    def arrived(buffer, sem, i):
        return pltpu.make_async_remote_copy(
            src_ref=buffer.at[i], dst_ref=buffer.at[i], send_sem=rs_send.at[0], recv_sem=sem.at[i],
            device_id=place(me, my_z), device_id_type=MESH,
        )

    def z_copy(d):
        return pltpu.make_async_remote_copy(
            src_ref=zrecv.at[my_z], dst_ref=zrecv.at[my_z], send_sem=z_send.at[d], recv_sem=z_recv.at[my_z],
            device_id=place(me, (my_z + d) % nz), device_id_type=MESH,
        )

    def ag_copy(d):
        return pltpu.make_async_remote_copy(
            src_ref=total.at[me], dst_ref=total.at[me], send_sem=ag_send.at[d], recv_sem=ag_recv.at[me],
            device_id=place((me + d) % plane, my_z), device_id_type=MESH,
        )

    def z_stage():
        def wait(d, carry):
            arrived(recv, rs_recv, (me + d) % plane).wait_recv()
            return carry

        lax.fori_loop(1, plane, wait, 0)
        parts = [recv[i] for i in range(plane)]
        while len(parts) > 1:
            parts = [parts[i] + parts[i + 1] for i in range(0, len(parts), 2)]
        zrecv[my_z] = parts[0]
        for i in range(nz // 2):
            for d in ((nz // 2,) if i == 0 else (nz // 2 - i, nz // 2 + i)):
                z_copy(d).start()

    def ag_stage():
        def wait(d, carry):
            arrived(zrecv, z_recv, (my_z + d) % nz).wait_recv()
            return carry

        lax.fori_loop(1, nz, wait, 0)
        parts = [zrecv[i] for i in range(nz)]
        while len(parts) > 1:
            parts = [parts[i] + parts[i + 1] for i in range(0, len(parts), 2)]
        total[me] = parts[0]

        def send(d, carry):
            ag_copy(d).start()
            return carry

        lax.fori_loop(1, plane, send, 0)

    def ag_wait(low, high):
        def wait(slot, carry):
            @pl.when(me != slot)
            def _():
                arrived(total, ag_recv, slot).wait_recv()

            return carry

        lax.fori_loop(low, high, wait, 0)

    owns_gram = owns_rest = None
    if comm:
        owns_gram = me < GSLOTS
        owns_rest = jnp.logical_and(me >= GSLOTS, me < SLOTS)
        pl.semaphore_wait(barrier, nz - 1 + plane - 1)
        rs_start(0, GSLOTS)

    accm[...] = jnp.zeros_like(accm)
    accc[...] = jnp.zeros_like(accc)
    accd[...] = jnp.zeros_like(accd)
    accv[...] = jnp.zeros_like(accv)

    def adjoint(c, slot):
        sums = [jnp.zeros((A, SUB), F32) for _ in range(7)]
        for b in range(width // SUB):
            at = pl.ds(pl.multiple_of(c * width + b * SUB, SUB), SUB)
            to = pl.ds(b * SUB, SUB)
            s, t = s_ref[:, at], t_ref[:, at]
            up, down, flat = pltpu.roll(s, A - 1, 0), pltpu.roll(s, 1, 0), 1.0 - t * t
            up_ref[:, at] = up
            down_ref[:, at] = down
            flat_ref[:, at] = flat
            spread = wide(0)
            e = 1.0 + s * spread
            drift = e * (z_ref[:, at] - spread)
            q = (drift - s) * wide(3)
            cf = cf_ref[:, at]
            for i, x in enumerate(
                (q, q * s, q * up, q * down, q * flat)
            ):
                hi, lo = split(x)
                q_ref[slot, i * A : (i + 1) * A, to] = hi
                q_ref[slot, (5 + i) * A : (6 + i) * A, to] = lo
                sums[i] = sums[i] + x * cf
            basket = jnp.sum(wide(4) * e, axis=0, keepdims=True)
            arg = (basket - 1.0) * (1.0 / soft_width)
            tiny = jnp.exp(-jnp.abs(arg))
            plus = jnp.maximum(arg, 0.0) + jnp.log1p(tiny)
            slope = jnp.where(arg >= 0.0, 1.0, tiny) / (1.0 + tiny)
            taken = 1.0 - free_ref[:, at]
            bar = taken * (notional * slope)
            rew_ref[:, at] = taken * (notional * soft_width * plus)
            bar_ref[:, at] = bar
            sums[5] = sums[5] + bar * (e - basket)
            sums[6] = sums[6] + bar * drift
        for i, x in enumerate(sums):
            folded = x[:, :128]
            for j in range(1, SUB // 128):
                folded = folded + x[:, j * 128 : (j + 1) * 128]
            if i < 5:
                accc[i * A : (i + 1) * A, :] += folded
            else:
                (accd, accv)[i - 5][...] += folded

    def rest_dot(slot, f_ref, half):
        f = f_ref[:, pl.ds(pl.multiple_of(half * width, width), width)]
        accm[...] += lax.dot_general(q_ref[slot], f, LAST, preferred_element_type=F32)

    def adjoint_step(i, carry):
        if comm:
            @pl.when(jnp.logical_and(owns_gram, i == pairs // 2))
            def _():
                z_stage()

        adjoint(2 * i + 1, 1)
        rest_dot(0, fe_ref, i)
        adjoint(2 * i + 2, 0)
        rest_dot(1, fo_ref, i)
        return carry

    adjoint(0, 0)
    lax.fori_loop(0, pairs - 1, adjoint_step, 0)
    adjoint(chunks - 1, 1)
    rest_dot(0, fe_ref, pairs - 1)
    rest_dot(1, fo_ref, pairs - 1)

    lowl = lax.broadcasted_iota(jnp.int32, (5 * A, N), 1) < N - 1
    right = accm[: 5 * A, N:] + accm[5 * A :, N:]
    rest = (accm[: 5 * A, :N] + accm[5 * A :, :N]) + jnp.where(lowl, right, 0.0)
    mfree = right[:, N - 1 : N]
    for j in range(20):
        pay[GSLOTS + j] = rest[8 * j : 8 * j + 8, :]
    lane8 = lax.broadcasted_iota(jnp.int32, (8, N), 1)
    cols = []
    dsum = jnp.sum(accd[...], axis=1, keepdims=True)
    vsum = jnp.sum(accv[...], axis=1, keepdims=True)
    mcf = jnp.sum(accc[...], axis=1, keepdims=True)
    for x, count in ((dsum, 4), (vsum, 4), (mcf, 20), (mfree, 20)):
        cols += [x[8 * i : 8 * i + 8, :] for i in range(count)]
    extra = jnp.zeros((8, N), F32)
    for i, x in enumerate(cols):
        extra = jnp.where(lane8 == i, x, extra)
    pay[SLOTS - 1] = extra

    if comm:
        rs_start(GSLOTS, SLOTS)

        @pl.when(owns_rest)
        def _():
            z_stage()

        @pl.when(owns_gram)
        def _():
            ag_stage()

        ag_wait(0, GSLOTS)
    else:
        total[...] = pay[...]

    per_path = 1.0 / total_paths
    packed = jnp.concatenate([total[j] for j in range(8)], axis=0)
    upper = jnp.where(lane > prow, packed, jnp.where(lane == prow, 0.5 * packed, 0.0))
    tail = total[8]
    lower = jnp.where(
        lane == prow, 0.5 * jnp.broadcast_to(tail[2:3, :], (N // 2, N)), jnp.where(lane < prow, packed, 0.0)
    )
    lower = pltpu.roll(jnp.where(lane < N // 2, lower, 0.0), N // 2, 1)
    folded = jnp.concatenate([upper, lower], axis=0) * per_path
    gram = folded + folded.T

    def between():
        if comm:
            @pl.when(owns_rest)
            def _():
                ag_stage()

    sol = solve(gram, jnp.where(r8 < 2, tail, 0.0) * per_path, between)
    reg, mult = sol[0:1, :], sol[1:2, :]
    big = lax.broadcasted_iota(jnp.int32, (N, N), 0)
    coef = jnp.where(big == 0, reg, jnp.where(big == 1, mult, 0.0)).T

    offsets = []
    for i in range(2):
        c1, c2, c3, c4 = (coef[A * b : A * (b + 1), i : i + 1] for b in range(4))
        c2 = c2 * inv_root_two
        c3d = jnp.concatenate([c3[A - 1 :], c3[: A - 1]], axis=0)
        for j, x in enumerate((c1, c2, c3, c3d, c4)):
            const[7 + 5 * i + j] = jnp.broadcast_to(x, (A, 128))
        offsets.append(jnp.sum(c2, axis=0, keepdims=True))

    def path_step(c, carry):
        for b in range(width // SUB):
            at = pl.ds(pl.multiple_of(c * width + b * SUB, SUB), SUB)
            s, t = s_ref[:, at], t_ref[:, at]
            up, down, flat = up_ref[:, at], down_ref[:, at], flat_ref[:, at]
            fits, bars = [], []
            for i in range(2):
                square = wide(8 + 5 * i) * s
                lead = wide(7 + 5 * i) + square + wide(9 + 5 * i) * up
                c4 = wide(11 + 5 * i)
                fits.append(jnp.sum(s * lead + c4 * t, axis=0, keepdims=True) - offsets[i])
                bars.append(lead + square + wide(10 + 5 * i) * down + c4 * flat)
            free = free_ref[:, at]
            cont, lam = fits
            value_ref[:, at] = rew_ref[:, at] + free * cont
            flow_ref[:, at] = lam
            cot_ref[:, at] = (
                wide(5) * ((cf_ref[:, at] - cont) * bars[1] + (free - lam) * bars[0]) + wide(6) * bar_ref[:, at]
            )
        return carry

    lax.fori_loop(0, chunks, path_step, 0)

    if comm:
        ag_wait(GSLOTS, SLOTS)
    extra = total[SLOTS - 1]
    vega = [jnp.zeros((8, 1), F32) for _ in range(4)]
    for kind in range(5):
        at = A * (kind if kind < 3 else kind - 1)
        cr, cm = coef[at : at + A, 0:1], coef[at : at + A, 1:2]
        if kind == 3:
            cr = jnp.concatenate([cr[A - 1 :], cr[: A - 1]], axis=0)
            cm = jnp.concatenate([cm[A - 1 :], cm[: A - 1]], axis=0)
        if kind == 1:
            cr, cm = cr * root_two, cm * root_two
        for i in range(4):
            j = 4 * kind + i
            block = total[GSLOTS + j]
            mr = extra[:, 8 + j : 9 + j] - jnp.sum(block * reg, axis=1, keepdims=True)
            mm = extra[:, 28 + j : 29 + j] - jnp.sum(block * mult, axis=1, keepdims=True)
            lo = 8 * i
            vega[i] = vega[i] + cm[lo : lo + 8] * mr + cr[lo : lo + 8] * mm
    delta = weight / whole * jnp.concatenate([extra[:, i : i + 1] for i in range(4)], axis=0)
    vrew = (root_time * share) * jnp.concatenate([extra[:, 4 + i : 5 + i] for i in range(4)], axis=0)
    vega = jnp.concatenate(vega, axis=0) + vrew
    glane = lax.broadcasted_iota(jnp.int32, (A, N), 1)
    both = jnp.where(glane == 0, delta, jnp.where(glane == 1, vega, 0.0)) * per_path
    both = jnp.concatenate([both, jnp.zeros((N - A, N), F32)], axis=0).T
    greek_out[...] = both[0:2, 0:A]

    if comm:
        def sent_slot(slot, carry):
            @pl.when(me != slot)
            def _():
                rs_copy(slot).wait_send()

            return carry

        lax.fori_loop(0, SLOTS, sent_slot, 0)

        @pl.when(me < SLOTS)
        def _():
            def sent_z(d, carry):
                z_copy(d).wait_send()
                return carry

            lax.fori_loop(1, nz, sent_z, 0)

            def sent_ag(d, carry):
                ag_copy(d).wait_send()
                return carry

            lax.fori_loop(1, plane, sent_ag, 0)


def second_kernel(value_ref, cot_ref, flow_ref, greek_ref, value_hbm, cot_hbm, flow_hbm, greek_hbm, sem):
    copies = [(value_ref, value_hbm), (flow_ref, flow_hbm), (greek_ref, greek_hbm)]
    copies = [(cot_ref.at[8 * i : 8 * i + 8], cot_hbm.at[8 * i : 8 * i + 8]) for i in range(A // 8)] + copies
    copies = [pltpu.make_async_copy(src, dst, sem.at[i]) for i, (src, dst) in enumerate(copies)]
    for copy in copies:
        copy.start()
    for copy in copies:
        copy.wait()


def per_device(dims, total_paths, normals, spot, vol, weights, cash_flows, exercise, width=2048):
    comm = dims is not None
    local = normals.shape[1]
    chunks = local // width
    spot, vol, weights = (x.reshape(1, A) for x in (spot, vol, weights))
    cash_flows, exercise = cash_flows.reshape(1, local), exercise.reshape(1, local)
    if comm:
        normals, spot, vol, weights, cash_flows, exercise = (
            pltpu.with_memory_space_constraint(x, pltpu.HBM)
            for x in (normals, spot, vol, weights, cash_flows, exercise)
        )
    vmem = pl.BlockSpec(memory_space=pltpu.VMEM)
    hbm = pl.BlockSpec(memory_space=pltpu.HBM)
    nz, plane = (dims[3], dims[0] * dims[1] * dims[2]) if comm else (2, 2)
    dma = pltpu.SemaphoreType.DMA
    wide, flat = jax.ShapeDtypeStruct((A, local), F32), jax.ShapeDtypeStruct((1, local), F32)
    half = pltpu.VMEM((2 * N, local // 2), BF16)
    tiny = pltpu.VMEM((1, A), F32)
    results = pl.pallas_call(
        functools.partial(first_kernel, dims, total_paths, width),
        out_shape=(flat, wide, flat, jax.ShapeDtypeStruct((2, A), F32)),
        in_specs=[hbm] * 6,
        out_specs=(vmem,) * 4,
        scratch_shapes=[
            *[pltpu.VMEM((A, local), F32)] * 5, *[pltpu.VMEM((1, local), F32)] * 4,
            pltpu.VMEM((A, local), F32), tiny, tiny, tiny, pltpu.VMEM((1, local), jnp.int32),
            half, half, pltpu.VMEM((16, local), BF16), pltpu.VMEM((2, 10 * A, width), BF16),
            pltpu.VMEM((17, A, 128), F32),
            pltpu.VMEM((2 * N, 2 * N), F32), pltpu.VMEM((16, 2 * N), F32),
            pltpu.VMEM((10 * A, 2 * N), F32), pltpu.VMEM((5 * A, 128), F32),
            pltpu.VMEM((A, 128), F32), pltpu.VMEM((A, 128), F32),
            pltpu.VMEM((SLOTS, 8, N), F32), pltpu.VMEM((plane, 8, N), F32),
            pltpu.VMEM((nz, 8, N), F32), pltpu.VMEM((SLOTS, 8, N), F32),
            dma((chunks,)), dma((5,)), dma((SLOTS,)), dma((plane,)),
            dma((nz,)), dma((nz,)), dma((plane,)), dma((SLOTS,)),
        ],
        compiler_params=pltpu.CompilerParams(
            has_side_effects=True, vmem_limit_bytes=40 * 2**20, **({"collective_id": 0} if comm else {})
        ),
        name="normal_equations",
    )(normals, spot, vol, weights, cash_flows, exercise)
    value, cot, flow, greeks = pl.pallas_call(
        second_kernel,
        out_shape=(flat, wide, flat, jax.ShapeDtypeStruct((2, A), F32)),
        in_specs=[vmem] * 4,
        out_specs=(hbm,) * 4,
        scratch_shapes=[dma((A // 8 + 3,))],
        compiler_params=pltpu.CompilerParams(vmem_limit_bytes=4 * 2**20),
        name="put_out",
    )(*results)
    return value.reshape(local), cot, flow.reshape(local), greeks


def solution(mesh):
    shape = dict(mesh.shape)
    ncore, ny = 2, 4
    dims = (shape["grp"] // ncore, ncore, ny, shape["path"] // ny)
    count = shape["grp"] * shape["path"]

    def body(normals, *rest):
        return per_device(dims, normals.shape[1] * count, normals, *rest)

    split_paths = ("grp", "path")
    in_specs = (P(None, split_paths), P(), P(), P(), P(split_paths), P(split_paths))
    out_specs = (P(split_paths), P(None, split_paths), P(split_paths), P())
    return jax.shard_map(body, mesh=mesh, in_specs=in_specs, out_specs=out_specs, check_vma=False)
```

```python
import functools
import math

import jax
import jax.numpy as jnp
from jax import lax
from jax.experimental import pallas as pl
from jax.experimental.pallas import tpu as pltpu
from jax.sharding import PartitionSpec as P

MESH = pl.DeviceIdType.MESH
F32, BF16 = jnp.float32, jnp.bfloat16
expiry_time = 0.5
root_time = math.sqrt(0.5)
inv_root_two = 1.0 / math.sqrt(2.0)
root_two = math.sqrt(2.0)
notional = 20.0
soft_width = 0.02
LAST = (((1,), (1,)), ((), ()))
A = 32
N = 4 * A
GSLOTS = 9
SUB = 256
SLOTS = 30


def column(row, size):
    eye = lax.broadcasted_iota(jnp.int32, (size, size), 0) == lax.broadcasted_iota(
        jnp.int32, (size, size), 1
    )
    return jnp.sum(jnp.where(eye, jnp.broadcast_to(row, (size, size)), 0.0), axis=1, keepdims=True)


def split(x):
    hi = x.astype(BF16)
    return hi, (x - hi.astype(F32)).astype(BF16)


def pivots(tile, k, lane):
    across = [jnp.broadcast_to(tile[:, k + j : k + j + 1], (8, N)) for j in range(4)]
    q0 = k % 8

    def at(i, j):
        return jnp.broadcast_to(across[j][q0 + i : q0 + i + 1, :], (8, N))

    a, h, c = at(0, 0), at(0, 1), at(1, 1)
    b00, b01, b10, b11 = at(0, 2), at(0, 3), at(1, 2), at(1, 3)
    d00, d01, d11 = at(2, 2), at(2, 3), at(3, 3)
    inv = 1.0 / (a * c - h * h)
    i00, i01, i11 = c * inv, -(h * inv), a * inv
    e00, e01 = i00 * b00 + i01 * b10, i00 * b01 + i01 * b11
    e10, e11 = i01 * b00 + i11 * b10, i01 * b01 + i11 * b11
    s00 = d00 - (b00 * e00 + b10 * e10)
    s01 = d01 - (b00 * e01 + b10 * e11)
    s11 = d11 - (b01 * e01 + b11 * e11)
    inv = 1.0 / (s00 * s11 - s01 * s01)
    w00, w01, w11 = s11 * inv, -(s01 * inv), s00 * inv
    r0, r1, r2, r3 = (
        jnp.broadcast_to(tile[q0 + q : q0 + q + 1, :], (8, N)) - (lane == k + q).astype(F32) for q in range(4)
    )
    t2 = r2 - (e00 * r0 + e10 * r1)
    t3 = r3 - (e01 * r0 + e11 * r1)
    low0 = w00 * t2 + w01 * t3
    low1 = w01 * t2 + w11 * t3
    up0 = (i00 * r0 + i01 * r1) - (e00 * low0 + e01 * low1)
    up1 = (i01 * r0 + i11 * r1) - (e10 * low0 + e11 * low1)
    return across, (up0, up1, low0, low1)


def take(x, k, w, across=None):
    c = across or [jnp.broadcast_to(x[:, k + q : k + q + 1], (8, N)) for q in range(4)]
    return x - ((c[0] * w[0] + c[1] * w[1]) + (c[2] * w[2] + c[3] * w[3]))


def solve(g, b, between):
    tiles = N // 8
    lane = lax.broadcasted_iota(jnp.int32, (8, N), 1)
    sub = lax.broadcasted_iota(jnp.int32, (8, N), 0)
    rows = [g[8 * i : 8 * i + 8, :] for i in range(tiles)] + [b]
    for t in range(tiles):
        if t == tiles // 2:
            between()
        k = 8 * t
        across, first = pivots(rows[t], k, lane)
        tile = take(rows[t], k, first, across)
        _, second = pivots(tile, k + 4, lane)
        rows[t + 1] = take(take(rows[t + 1], k, first), k + 4, second)
        if t + 2 <= tiles:
            w = jnp.where(sub < 2, jnp.where(sub < 1, first[0], first[1]), jnp.where(sub < 3, first[2], first[3]))
            w = take(jnp.where(sub < 4, w, 0.0), k + 4, second)
            low = jnp.where(sub < 6, jnp.where(sub < 5, second[0], second[1]), jnp.where(sub < 7, second[2], second[3]))
            w = jnp.where(sub < 4, w, low)
            parts = [w]
            if t > 0:
                parts = [jnp.zeros((k, N), F32)] + parts
            if t + 1 < tiles:
                parts = parts + [jnp.zeros((N - k - 8, N), F32)]
            change = jnp.dot(
                jnp.concatenate(rows[t + 2 :], axis=0), jnp.concatenate(parts, axis=0),
                precision=lax.Precision.HIGHEST, preferred_element_type=F32,
            )
            for i in range(t + 2, tiles + 1):
                j = 8 * (i - t - 2)
                rows[i] = rows[i] - change[j : j + 8, :]
    return rows[tiles]


def first_kernel(
    dims, total_paths, width,
    z_hbm, spot_hbm, vol_hbm, wei_hbm, cf_hbm, ex_hbm,
    value_ref, cot_ref, flow_ref, greek_out,
    s_ref, t_ref, up_ref, down_ref, flat_ref, cf_ref, free_ref, rew_ref, bar_ref, z_ref, spot_ref, vol_ref, wei_ref, ex_ref, fe_ref, fo_ref, tar_ref, q_ref, const,
    acc, acct, accm, accc, accd, accv,
    pay, recv, zrecv, total,
    in_sem, par_sem, rs_send, rs_recv, z_send, z_recv, ag_send, ag_recv,
):
    local = z_ref.shape[1]
    chunks = local // width
    comm = dims is not None
    if comm:
        nx, ncore, ny, nz = dims
        plane = nx * ncore * ny
        grp, path = lax.axis_index("grp"), lax.axis_index("path")
        my_z, my_y = path // ny, path % ny
        my_x, my_core = grp // ncore, grp % ncore
        me = (my_core * ny + my_y) * nx + my_x

        def place(slot, z):
            x, y, core = slot % nx, (slot // nx) % ny, slot // (nx * ny)
            return (x * ncore + core, z * ny + y)

        barrier = pltpu.get_barrier_semaphore()

        def greet_z(d, carry):
            peer = place(me, (my_z + d) % nz)
            pl.semaphore_signal(barrier, inc=1, device_id=peer, device_id_type=MESH)
            return carry

        def greet_plane(d, carry):
            peer = place((me + d) % plane, my_z)
            pl.semaphore_signal(barrier, inc=1, device_id=peer, device_id_type=MESH)
            return carry


    def in_copy(c):
        at = pl.ds(pl.multiple_of(c * width, width), width)
        return pltpu.make_async_copy(z_hbm.at[:, at], z_ref.at[:, at], in_sem.at[c])

    small = [
        pltpu.make_async_copy(src, dst, par_sem.at[i])
        for i, (src, dst) in enumerate(
            ((spot_hbm, spot_ref), (vol_hbm, vol_ref), (wei_hbm, wei_ref), (cf_hbm, cf_ref), (ex_hbm, ex_ref))
        )
    ]
    for i in (1, 0, 2):
        small[i].start()
    in_copy(0).start()
    small[3].start()
    small[4].start()
    for c in range(1, chunks):
        in_copy(c).start()
    if comm:
        lax.fori_loop(1, nz, greet_z, 0)
        lax.fori_loop(1, plane, greet_plane, 0)
    for i in range(3):
        small[i].wait()

    vol = column(vol_ref[...], A)
    spot = column(spot_ref[...], A)
    weight = column(wei_ref[...], A)
    spread = vol * root_time
    whole = jnp.sum(weight * spot, axis=0, keepdims=True)
    share = weight * spot / whole
    for i, x in enumerate(
        (spread, 0.5 * expiry_time * (vol * vol), 1.0 / spread, 1.0 / vol, share, 1.0 / (spot * spread), weight / whole)
    ):
        const[i] = jnp.broadcast_to(x, (A, 128))

    def wide(i):
        x = const[i]
        return jnp.concatenate([x] * (SUB // 128), axis=1)

    row = lax.broadcasted_iota(jnp.int32, (A, SUB), 0)
    trow = lax.broadcasted_iota(jnp.int32, (16, SUB), 0)

    acc[...] = jnp.zeros_like(acc)
    acct[...] = jnp.zeros_like(acct)
    small[3].wait()
    small[4].wait()

    def basis(c, f_ref, half):
        in_copy(c).wait()
        for b in range(width // SUB):
            at = pl.ds(pl.multiple_of(c * width + b * SUB, SUB), SUB)
            to = pl.ds(pl.multiple_of(half * width + b * SUB, SUB), SUB)
            e = jnp.exp(wide(0) * z_ref[:, at] - wide(1))
            s = (e - 1.0) * wide(2)
            t = jnp.where(row == A - 1, 1.0, jnp.tanh(s))
            s_ref[:, at] = s
            t_ref[:, at] = t
            free = 1.0 - ex_ref[:, at].astype(F32)
            free_ref[:, at] = free
            blocks = (s, (s * s - 1.0) * inv_root_two, s * pltpu.roll(s, A - 1, 0), t)
            for i, x in enumerate(blocks):
                hi, lo = split(x)
                if i == 3:
                    lo = (x - hi.astype(F32))
                    lo = jnp.where(row == A - 1, jnp.broadcast_to(free, (A, SUB)), lo).astype(BF16)
                f_ref[i * A : (i + 1) * A, to] = hi
                f_ref[N + i * A : N + (i + 1) * A, to] = lo
            cf = jnp.broadcast_to(cf_ref[:, at], (16, SUB))
            c0 = cf.astype(BF16).astype(F32)
            c1 = (cf - c0).astype(BF16).astype(F32)
            c2 = cf - c0 - c1
            tar_ref[:, at] = jnp.where(
                trow == 0, c0, jnp.where(trow == 1, c1, jnp.where(trow == 2, c2, 0.0))
            ).astype(BF16)

    def gram_dot(c, f_ref, half):
        f = f_ref[:, pl.ds(pl.multiple_of(half * width, width), width)]
        acc[...] += lax.dot_general(f, f, LAST, preferred_element_type=F32)
        at = pl.ds(pl.multiple_of(c * width, width), width)
        acct[...] += lax.dot_general(tar_ref[:, at], f, LAST, preferred_element_type=F32)

    pairs = chunks // 2
    basis(0, fe_ref, 0)

    def gram_step(i, carry):
        basis(2 * i + 1, fo_ref, i)
        gram_dot(2 * i, fe_ref, i)
        basis(2 * i + 2, fe_ref, i + 1)
        gram_dot(2 * i + 1, fo_ref, i)
        return carry

    lax.fori_loop(0, pairs - 1, gram_step, 0)
    basis(chunks - 1, fo_ref, pairs - 1)
    gram_dot(chunks - 2, fe_ref, pairs - 1)
    gram_dot(chunks - 1, fo_ref, pairs - 1)

    low_row = lax.broadcasted_iota(jnp.int32, (N, N), 0) < N - 1
    low_col = lax.broadcasted_iota(jnp.int32, (N, N), 1) < N - 1
    cross = jnp.where(low_col, acc[:N, N:], 0.0) + jnp.where(low_row, acc[N:, :N], 0.0)
    gram = (acc[:N, :N] + cross) + jnp.where(jnp.logical_and(low_row, low_col), acc[N:, N:], 0.0)
    lane1 = lax.broadcasted_iota(jnp.int32, (16, N), 1)
    moment = acct[:, :N] + jnp.where(lane1 < N - 1, acct[:, N:], 0.0)
    lane1 = lax.broadcasted_iota(jnp.int32, (1, N), 1)
    moment_free = acc[2 * N - 1 :, :N] + jnp.where(lane1 < N - 1, acc[2 * N - 1 :, N:], 0.0)
    lane = lax.broadcasted_iota(jnp.int32, (N // 2, N), 1)
    prow = lax.broadcasted_iota(jnp.int32, (N // 2, N), 0)
    corner = pltpu.roll(gram[N // 2 :, :], N // 2, 1)
    packed = jnp.where(lane < prow, corner, gram[: N // 2, :])
    diagonal = jnp.sum(jnp.where(lane == prow, corner, 0.0), axis=0, keepdims=True)
    for j in range(8):
        pay[j] = packed[8 * j : 8 * j + 8, :]
    r8 = lax.broadcasted_iota(jnp.int32, (8, N), 0)
    pay[8] = jnp.where(
        r8 == 0,
        moment[0:1, :] + moment[1:2, :] + moment[2:3, :],
        jnp.where(r8 == 1, moment_free, jnp.where(r8 == 2, diagonal, 0.0)),
    )

    def rs_copy(slot):
        return pltpu.make_async_remote_copy(
            src_ref=pay.at[slot], dst_ref=recv.at[me], send_sem=rs_send.at[slot], recv_sem=rs_recv.at[me],
            device_id=place(slot, my_z), device_id_type=MESH,
        )

    def rs_start(low, high):
        for slot in range(low, high):
            @pl.when(me != slot)
            def _():
                rs_copy(slot).start()

            @pl.when(me == slot)
            def _():
                recv[me] = pay[slot]

    def arrived(buffer, sem, i):
        return pltpu.make_async_remote_copy(
            src_ref=buffer.at[i], dst_ref=buffer.at[i], send_sem=rs_send.at[0], recv_sem=sem.at[i],
            device_id=place(me, my_z), device_id_type=MESH,
        )

    def z_copy(d):
        return pltpu.make_async_remote_copy(
            src_ref=zrecv.at[my_z], dst_ref=zrecv.at[my_z], send_sem=z_send.at[d], recv_sem=z_recv.at[my_z],
            device_id=place(me, (my_z + d) % nz), device_id_type=MESH,
        )

    def ag_copy(slot):
        return pltpu.make_async_remote_copy(
            src_ref=total.at[me], dst_ref=total.at[me], send_sem=ag_send.at[slot], recv_sem=ag_recv.at[me],
            device_id=place(slot, my_z), device_id_type=MESH,
        )

    def z_stage():
        def wait(d, carry):
            arrived(recv, rs_recv, (me + d) % plane).wait_recv()
            return carry

        lax.fori_loop(1, plane, wait, 0)
        parts = [recv[i] for i in range(plane)]
        while len(parts) > 1:
            parts = [parts[i] + parts[i + 1] for i in range(0, len(parts), 2)]
        zrecv[my_z] = parts[0]
        for i in range(nz // 2):
            for d in ((nz // 2,) if i == 0 else (nz // 2 - i, nz // 2 + i)):
                z_copy(d).start()

    def ag_stage():
        def wait(d, carry):
            arrived(zrecv, z_recv, (my_z + d) % nz).wait_recv()
            return carry

        lax.fori_loop(1, nz, wait, 0)
        parts = [zrecv[i] for i in range(nz)]
        while len(parts) > 1:
            parts = [parts[i] + parts[i + 1] for i in range(0, len(parts), 2)]
        total[me] = parts[0]

        for slot in range(plane):
            @pl.when(me != slot)
            def _():
                ag_copy(slot).start()

    def ag_wait(low, high):
        def wait(slot, carry):
            @pl.when(me != slot)
            def _():
                arrived(total, ag_recv, slot).wait_recv()

            return carry

        lax.fori_loop(low, high, wait, 0)

    owns_gram = owns_rest = None
    if comm:
        owns_gram = me < GSLOTS
        owns_rest = jnp.logical_and(me >= GSLOTS, me < SLOTS)
        pl.semaphore_wait(barrier, nz - 1 + plane - 1)
        rs_start(0, GSLOTS)

    accm[...] = jnp.zeros_like(accm)
    accc[...] = jnp.zeros_like(accc)
    accd[...] = jnp.zeros_like(accd)
    accv[...] = jnp.zeros_like(accv)

    def adjoint(c, slot):
        sums = [jnp.zeros((A, SUB), F32) for _ in range(7)]
        for b in range(width // SUB):
            at = pl.ds(pl.multiple_of(c * width + b * SUB, SUB), SUB)
            to = pl.ds(b * SUB, SUB)
            s, t = s_ref[:, at], t_ref[:, at]
            up, down, flat = pltpu.roll(s, A - 1, 0), pltpu.roll(s, 1, 0), 1.0 - t * t
            up_ref[:, at] = up
            down_ref[:, at] = down
            flat_ref[:, at] = flat
            spread = wide(0)
            e = 1.0 + s * spread
            drift = e * (z_ref[:, at] - spread)
            q = (drift - s) * wide(3)
            cf = cf_ref[:, at]
            for i, x in enumerate(
                (q, q * s, q * up, q * down, q * flat)
            ):
                hi, lo = split(x)
                q_ref[slot, i * A : (i + 1) * A, to] = hi
                q_ref[slot, (5 + i) * A : (6 + i) * A, to] = lo
                sums[i] = sums[i] + x * cf
            basket = jnp.sum(wide(4) * e, axis=0, keepdims=True)
            arg = (basket - 1.0) * (1.0 / soft_width)
            tiny = jnp.exp(-jnp.abs(arg))
            plus = jnp.maximum(arg, 0.0) + jnp.log1p(tiny)
            slope = jnp.where(arg >= 0.0, 1.0, tiny) / (1.0 + tiny)
            taken = 1.0 - free_ref[:, at]
            bar = taken * (notional * slope)
            rew_ref[:, at] = taken * (notional * soft_width * plus)
            bar_ref[:, at] = bar
            sums[5] = sums[5] + bar * (e - basket)
            sums[6] = sums[6] + bar * drift
        for i, x in enumerate(sums):
            folded = x[:, :128]
            for j in range(1, SUB // 128):
                folded = folded + x[:, j * 128 : (j + 1) * 128]
            if i < 5:
                accc[i * A : (i + 1) * A, :] += folded
            else:
                (accd, accv)[i - 5][...] += folded

    def rest_dot(slot, f_ref, half):
        f = f_ref[:, pl.ds(pl.multiple_of(half * width, width), width)]
        accm[...] += lax.dot_general(q_ref[slot], f, LAST, preferred_element_type=F32)

    def adjoint_step(i, carry):
        if comm:
            @pl.when(jnp.logical_and(owns_gram, i == pairs // 2))
            def _():
                z_stage()

        adjoint(2 * i + 1, 1)
        rest_dot(0, fe_ref, i)
        adjoint(2 * i + 2, 0)
        rest_dot(1, fo_ref, i)
        return carry

    adjoint(0, 0)
    lax.fori_loop(0, pairs - 1, adjoint_step, 0)
    adjoint(chunks - 1, 1)
    rest_dot(0, fe_ref, pairs - 1)
    rest_dot(1, fo_ref, pairs - 1)

    lowl = lax.broadcasted_iota(jnp.int32, (5 * A, N), 1) < N - 1
    right = accm[: 5 * A, N:] + accm[5 * A :, N:]
    rest = (accm[: 5 * A, :N] + accm[5 * A :, :N]) + jnp.where(lowl, right, 0.0)
    mfree = right[:, N - 1 : N]
    for j in range(20):
        pay[GSLOTS + j] = rest[8 * j : 8 * j + 8, :]
    lane8 = lax.broadcasted_iota(jnp.int32, (8, N), 1)
    cols = []
    dsum = jnp.sum(accd[...], axis=1, keepdims=True)
    vsum = jnp.sum(accv[...], axis=1, keepdims=True)
    mcf = jnp.sum(accc[...], axis=1, keepdims=True)
    for x, count in ((dsum, 4), (vsum, 4), (mcf, 20), (mfree, 20)):
        cols += [x[8 * i : 8 * i + 8, :] for i in range(count)]
    extra = jnp.zeros((8, N), F32)
    for i, x in enumerate(cols):
        extra = jnp.where(lane8 == i, x, extra)
    pay[SLOTS - 1] = extra

    if comm:
        rs_start(GSLOTS, SLOTS)

        @pl.when(owns_rest)
        def _():
            z_stage()

        @pl.when(owns_gram)
        def _():
            ag_stage()

        ag_wait(0, GSLOTS)
    else:
        total[...] = pay[...]

    per_path = 1.0 / total_paths
    packed = jnp.concatenate([total[j] for j in range(8)], axis=0)
    upper = jnp.where(lane > prow, packed, jnp.where(lane == prow, 0.5 * packed, 0.0))
    tail = total[8]
    lower = jnp.where(
        lane == prow, 0.5 * jnp.broadcast_to(tail[2:3, :], (N // 2, N)), jnp.where(lane < prow, packed, 0.0)
    )
    lower = pltpu.roll(jnp.where(lane < N // 2, lower, 0.0), N // 2, 1)
    folded = jnp.concatenate([upper, lower], axis=0) * per_path
    gram = folded + folded.T

    def between():
        if comm:
            @pl.when(owns_rest)
            def _():
                ag_stage()

    sol = solve(gram, jnp.where(r8 < 2, tail, 0.0) * per_path, between)
    reg, mult = sol[0:1, :], sol[1:2, :]
    big = lax.broadcasted_iota(jnp.int32, (N, N), 0)
    coef = jnp.where(big == 0, reg, jnp.where(big == 1, mult, 0.0)).T

    offsets = []
    for i in range(2):
        c1, c2, c3, c4 = (coef[A * b : A * (b + 1), i : i + 1] for b in range(4))
        c2 = c2 * inv_root_two
        c3d = jnp.concatenate([c3[A - 1 :], c3[: A - 1]], axis=0)
        for j, x in enumerate((c1, c2, c3, c3d, c4)):
            const[7 + 5 * i + j] = jnp.broadcast_to(x, (A, 128))
        offsets.append(jnp.sum(c2, axis=0, keepdims=True))

    def path_step(c, carry):
        for b in range(width // SUB):
            at = pl.ds(pl.multiple_of(c * width + b * SUB, SUB), SUB)
            s, t = s_ref[:, at], t_ref[:, at]
            up, down, flat = up_ref[:, at], down_ref[:, at], flat_ref[:, at]
            fits, bars = [], []
            for i in range(2):
                square = wide(8 + 5 * i) * s
                lead = wide(7 + 5 * i) + square + wide(9 + 5 * i) * up
                c4 = wide(11 + 5 * i)
                fits.append(jnp.sum(s * lead + c4 * t, axis=0, keepdims=True) - offsets[i])
                bars.append(lead + square + wide(10 + 5 * i) * down + c4 * flat)
            free = free_ref[:, at]
            cont, lam = fits
            value_ref[:, at] = rew_ref[:, at] + free * cont
            flow_ref[:, at] = lam
            cot_ref[:, at] = (
                wide(5) * ((cf_ref[:, at] - cont) * bars[1] + (free - lam) * bars[0]) + wide(6) * bar_ref[:, at]
            )
        return carry

    lax.fori_loop(0, chunks, path_step, 0)

    if comm:
        ag_wait(GSLOTS, SLOTS)
    extra = total[SLOTS - 1]
    vega = [jnp.zeros((8, 1), F32) for _ in range(4)]
    for kind in range(5):
        at = A * (kind if kind < 3 else kind - 1)
        cr, cm = coef[at : at + A, 0:1], coef[at : at + A, 1:2]
        if kind == 3:
            cr = jnp.concatenate([cr[A - 1 :], cr[: A - 1]], axis=0)
            cm = jnp.concatenate([cm[A - 1 :], cm[: A - 1]], axis=0)
        if kind == 1:
            cr, cm = cr * root_two, cm * root_two
        for i in range(4):
            j = 4 * kind + i
            block = total[GSLOTS + j]
            mr = extra[:, 8 + j : 9 + j] - jnp.sum(block * reg, axis=1, keepdims=True)
            mm = extra[:, 28 + j : 29 + j] - jnp.sum(block * mult, axis=1, keepdims=True)
            lo = 8 * i
            vega[i] = vega[i] + cm[lo : lo + 8] * mr + cr[lo : lo + 8] * mm
    delta = weight / whole * jnp.concatenate([extra[:, i : i + 1] for i in range(4)], axis=0)
    vrew = (root_time * share) * jnp.concatenate([extra[:, 4 + i : 5 + i] for i in range(4)], axis=0)
    vega = jnp.concatenate(vega, axis=0) + vrew
    glane = lax.broadcasted_iota(jnp.int32, (A, N), 1)
    both = jnp.where(glane == 0, delta, jnp.where(glane == 1, vega, 0.0)) * per_path
    both = jnp.concatenate([both, jnp.zeros((N - A, N), F32)], axis=0).T
    greek_out[...] = both[0:2, 0:A]

    if comm:
        def sent_slot(slot, carry):
            @pl.when(me != slot)
            def _():
                rs_copy(slot).wait_send()

            return carry

        lax.fori_loop(0, SLOTS, sent_slot, 0)

        @pl.when(me < SLOTS)
        def _():
            def sent_z(d, carry):
                z_copy(d).wait_send()
                return carry

            lax.fori_loop(1, nz, sent_z, 0)

            def sent_ag(slot, carry):
                @pl.when(me != slot)
                def _():
                    ag_copy(slot).wait_send()

                return carry

            lax.fori_loop(0, plane, sent_ag, 0)


def second_kernel(value_ref, cot_ref, flow_ref, greek_ref, value_hbm, cot_hbm, flow_hbm, greek_hbm, sem):
    copies = [(value_ref, value_hbm), (flow_ref, flow_hbm), (greek_ref, greek_hbm)]
    copies = [(cot_ref.at[8 * i : 8 * i + 8], cot_hbm.at[8 * i : 8 * i + 8]) for i in range(A // 8)] + copies
    copies = [pltpu.make_async_copy(src, dst, sem.at[i]) for i, (src, dst) in enumerate(copies)]
    for copy in copies:
        copy.start()
    for copy in copies:
        copy.wait()


def per_device(dims, total_paths, normals, spot, vol, weights, cash_flows, exercise, width=2048):
    comm = dims is not None
    local = normals.shape[1]
    chunks = local // width
    spot, vol, weights = (x.reshape(1, A) for x in (spot, vol, weights))
    cash_flows, exercise = cash_flows.reshape(1, local), exercise.reshape(1, local)
    if comm:
        normals, spot, vol, weights, cash_flows, exercise = (
            pltpu.with_memory_space_constraint(x, pltpu.HBM)
            for x in (normals, spot, vol, weights, cash_flows, exercise)
        )
    vmem = pl.BlockSpec(memory_space=pltpu.VMEM)
    hbm = pl.BlockSpec(memory_space=pltpu.HBM)
    nz, plane = (dims[3], dims[0] * dims[1] * dims[2]) if comm else (2, 2)
    dma = pltpu.SemaphoreType.DMA
    wide, flat = jax.ShapeDtypeStruct((A, local), F32), jax.ShapeDtypeStruct((1, local), F32)
    half = pltpu.VMEM((2 * N, local // 2), BF16)
    tiny = pltpu.VMEM((1, A), F32)
    results = pl.pallas_call(
        functools.partial(first_kernel, dims, total_paths, width),
        out_shape=(flat, wide, flat, jax.ShapeDtypeStruct((2, A), F32)),
        in_specs=[hbm] * 6,
        out_specs=(vmem,) * 4,
        scratch_shapes=[
            *[pltpu.VMEM((A, local), F32)] * 5, *[pltpu.VMEM((1, local), F32)] * 4,
            pltpu.VMEM((A, local), F32), tiny, tiny, tiny, pltpu.VMEM((1, local), jnp.int32),
            half, half, pltpu.VMEM((16, local), BF16), pltpu.VMEM((2, 10 * A, width), BF16),
            pltpu.VMEM((17, A, 128), F32),
            pltpu.VMEM((2 * N, 2 * N), F32), pltpu.VMEM((16, 2 * N), F32),
            pltpu.VMEM((10 * A, 2 * N), F32), pltpu.VMEM((5 * A, 128), F32),
            pltpu.VMEM((A, 128), F32), pltpu.VMEM((A, 128), F32),
            pltpu.VMEM((SLOTS, 8, N), F32), pltpu.VMEM((plane, 8, N), F32),
            pltpu.VMEM((nz, 8, N), F32), pltpu.VMEM((SLOTS, 8, N), F32),
            dma((chunks,)), dma((5,)), dma((SLOTS,)), dma((plane,)),
            dma((nz,)), dma((nz,)), dma((plane,)), dma((SLOTS,)),
        ],
        compiler_params=pltpu.CompilerParams(
            has_side_effects=True, vmem_limit_bytes=40 * 2**20, **({"collective_id": 0} if comm else {})
        ),
        name="normal_equations",
    )(normals, spot, vol, weights, cash_flows, exercise)
    value, cot, flow, greeks = pl.pallas_call(
        second_kernel,
        out_shape=(flat, wide, flat, jax.ShapeDtypeStruct((2, A), F32)),
        in_specs=[vmem] * 4,
        out_specs=(hbm,) * 4,
        scratch_shapes=[dma((A // 8 + 3,))],
        compiler_params=pltpu.CompilerParams(vmem_limit_bytes=4 * 2**20),
        name="put_out",
    )(*results)
    return value.reshape(local), cot, flow.reshape(local), greeks


def solution(mesh):
    shape = dict(mesh.shape)
    ncore, ny = 2, 4
    dims = (shape["grp"] // ncore, ncore, ny, shape["path"] // ny)
    count = shape["grp"] * shape["path"]

    def body(normals, *rest):
        return per_device(dims, normals.shape[1] * count, normals, *rest)

    split_paths = ("grp", "path")
    in_specs = (P(None, split_paths), P(), P(), P(), P(split_paths), P(split_paths))
    out_specs = (P(split_paths), P(None, split_paths), P(split_paths), P())
    return jax.shard_map(body, mesh=mesh, in_specs=in_specs, out_specs=out_specs, check_vma=False)
```

```python
import functools
import math

import jax
import jax.numpy as jnp
from jax import lax
from jax.experimental import pallas as pl
from jax.experimental.pallas import tpu as pltpu
from jax.sharding import PartitionSpec as P

MESH = pl.DeviceIdType.MESH
F32, BF16 = jnp.float32, jnp.bfloat16
expiry_time = 0.5
root_time = math.sqrt(0.5)
inv_root_two = 1.0 / math.sqrt(2.0)
root_two = math.sqrt(2.0)
notional = 20.0
soft_width = 0.02
LAST = (((1,), (1,)), ((), ()))
A = 32
N = 4 * A
GSLOTS = 9
SUB = 512
SLOTS = 30


def column(row, size):
    eye = lax.broadcasted_iota(jnp.int32, (size, size), 0) == lax.broadcasted_iota(
        jnp.int32, (size, size), 1
    )
    return jnp.sum(jnp.where(eye, jnp.broadcast_to(row, (size, size)), 0.0), axis=1, keepdims=True)


def split(x):
    hi = x.astype(BF16)
    return hi, (x - hi.astype(F32)).astype(BF16)


def pivots(tile, k, lane):
    across = [jnp.broadcast_to(tile[:, k + j : k + j + 1], (8, N)) for j in range(4)]
    q0 = k % 8

    def at(i, j):
        return jnp.broadcast_to(across[j][q0 + i : q0 + i + 1, :], (8, N))

    a, h, c = at(0, 0), at(0, 1), at(1, 1)
    b00, b01, b10, b11 = at(0, 2), at(0, 3), at(1, 2), at(1, 3)
    d00, d01, d11 = at(2, 2), at(2, 3), at(3, 3)
    inv = 1.0 / (a * c - h * h)
    i00, i01, i11 = c * inv, -(h * inv), a * inv
    e00, e01 = i00 * b00 + i01 * b10, i00 * b01 + i01 * b11
    e10, e11 = i01 * b00 + i11 * b10, i01 * b01 + i11 * b11
    s00 = d00 - (b00 * e00 + b10 * e10)
    s01 = d01 - (b00 * e01 + b10 * e11)
    s11 = d11 - (b01 * e01 + b11 * e11)
    inv = 1.0 / (s00 * s11 - s01 * s01)
    w00, w01, w11 = s11 * inv, -(s01 * inv), s00 * inv
    r0, r1, r2, r3 = (
        jnp.broadcast_to(tile[q0 + q : q0 + q + 1, :], (8, N)) - (lane == k + q).astype(F32) for q in range(4)
    )
    t2 = r2 - (e00 * r0 + e10 * r1)
    t3 = r3 - (e01 * r0 + e11 * r1)
    low0 = w00 * t2 + w01 * t3
    low1 = w01 * t2 + w11 * t3
    up0 = (i00 * r0 + i01 * r1) - (e00 * low0 + e01 * low1)
    up1 = (i01 * r0 + i11 * r1) - (e10 * low0 + e11 * low1)
    return across, (up0, up1, low0, low1)


def take(x, k, w, across=None):
    c = across or [jnp.broadcast_to(x[:, k + q : k + q + 1], (8, N)) for q in range(4)]
    return x - ((c[0] * w[0] + c[1] * w[1]) + (c[2] * w[2] + c[3] * w[3]))


def solve(g, b, between):
    tiles = N // 8
    lane = lax.broadcasted_iota(jnp.int32, (8, N), 1)
    sub = lax.broadcasted_iota(jnp.int32, (8, N), 0)
    rows = [g[8 * i : 8 * i + 8, :] for i in range(tiles)] + [b]
    for t in range(tiles):
        if t == tiles // 2:
            between()
        k = 8 * t
        across, first = pivots(rows[t], k, lane)
        tile = take(rows[t], k, first, across)
        _, second = pivots(tile, k + 4, lane)
        rows[t + 1] = take(take(rows[t + 1], k, first), k + 4, second)
        if t + 2 <= tiles:
            w = jnp.where(sub < 2, jnp.where(sub < 1, first[0], first[1]), jnp.where(sub < 3, first[2], first[3]))
            w = take(jnp.where(sub < 4, w, 0.0), k + 4, second)
            low = jnp.where(sub < 6, jnp.where(sub < 5, second[0], second[1]), jnp.where(sub < 7, second[2], second[3]))
            w = jnp.where(sub < 4, w, low)
            parts = [w]
            if t > 0:
                parts = [jnp.zeros((k, N), F32)] + parts
            if t + 1 < tiles:
                parts = parts + [jnp.zeros((N - k - 8, N), F32)]
            change = jnp.dot(
                jnp.concatenate(rows[t + 2 :], axis=0), jnp.concatenate(parts, axis=0),
                precision=lax.Precision.HIGHEST, preferred_element_type=F32,
            )
            for i in range(t + 2, tiles + 1):
                j = 8 * (i - t - 2)
                rows[i] = rows[i] - change[j : j + 8, :]
    return rows[tiles]


def first_kernel(
    dims, total_paths, width,
    z_hbm, spot_hbm, vol_hbm, wei_hbm, cf_hbm, ex_hbm,
    value_ref, cot_ref, flow_ref, greek_out,
    s_ref, t_ref, up_ref, down_ref, flat_ref, cf_ref, free_ref, rew_ref, bar_ref, z_ref, spot_ref, vol_ref, wei_ref, ex_ref, fe_ref, fo_ref, tar_ref, q_ref, const,
    acc, acct, accm, accc, accd, accv,
    pay, recv, zrecv, total,
    in_sem, par_sem, rs_send, rs_recv, z_send, z_recv, ag_send, ag_recv,
):
    local = z_ref.shape[1]
    chunks = local // width
    comm = dims is not None
    if comm:
        nx, ncore, ny, nz = dims
        plane = nx * ncore * ny
        grp, path = lax.axis_index("grp"), lax.axis_index("path")
        my_z, my_y = path // ny, path % ny
        my_x, my_core = grp // ncore, grp % ncore
        me = (my_core * ny + my_y) * nx + my_x

        def place(slot, z):
            x, y, core = slot % nx, (slot // nx) % ny, slot // (nx * ny)
            return (x * ncore + core, z * ny + y)

        barrier = pltpu.get_barrier_semaphore()

        def greet_z(d, carry):
            peer = place(me, (my_z + d) % nz)
            pl.semaphore_signal(barrier, inc=1, device_id=peer, device_id_type=MESH)
            return carry

        def greet_plane(d, carry):
            peer = place((me + d) % plane, my_z)
            pl.semaphore_signal(barrier, inc=1, device_id=peer, device_id_type=MESH)
            return carry


    def in_copy(c):
        at = pl.ds(pl.multiple_of(c * width, width), width)
        return pltpu.make_async_copy(z_hbm.at[:, at], z_ref.at[:, at], in_sem.at[c])

    small = [
        pltpu.make_async_copy(src, dst, par_sem.at[i])
        for i, (src, dst) in enumerate(
            ((spot_hbm, spot_ref), (vol_hbm, vol_ref), (wei_hbm, wei_ref), (cf_hbm, cf_ref), (ex_hbm, ex_ref))
        )
    ]
    for i in (1, 0, 2):
        small[i].start()
    in_copy(0).start()
    small[3].start()
    small[4].start()
    for c in range(1, chunks):
        in_copy(c).start()
    if comm:
        lax.fori_loop(1, nz, greet_z, 0)
        lax.fori_loop(1, plane, greet_plane, 0)
    for i in range(3):
        small[i].wait()

    vol = column(vol_ref[...], A)
    spot = column(spot_ref[...], A)
    weight = column(wei_ref[...], A)
    spread = vol * root_time
    whole = jnp.sum(weight * spot, axis=0, keepdims=True)
    share = weight * spot / whole
    for i, x in enumerate(
        (spread, 0.5 * expiry_time * (vol * vol), 1.0 / spread, 1.0 / vol, share, 1.0 / (spot * spread), weight / whole)
    ):
        const[i] = jnp.broadcast_to(x, (A, 128))

    def wide(i):
        x = const[i]
        return jnp.concatenate([x] * (SUB // 128), axis=1)

    row = lax.broadcasted_iota(jnp.int32, (A, SUB), 0)
    trow = lax.broadcasted_iota(jnp.int32, (16, SUB), 0)

    acc[...] = jnp.zeros_like(acc)
    acct[...] = jnp.zeros_like(acct)
    small[3].wait()
    small[4].wait()

    def basis(c, f_ref, half):
        in_copy(c).wait()
        for b in range(width // SUB):
            at = pl.ds(pl.multiple_of(c * width + b * SUB, SUB), SUB)
            to = pl.ds(pl.multiple_of(half * width + b * SUB, SUB), SUB)
            e = jnp.exp(wide(0) * z_ref[:, at] - wide(1))
            s = (e - 1.0) * wide(2)
            t = jnp.where(row == A - 1, 1.0, jnp.tanh(s))
            s_ref[:, at] = s
            t_ref[:, at] = t
            free = 1.0 - ex_ref[:, at].astype(F32)
            free_ref[:, at] = free
            blocks = (s, (s * s - 1.0) * inv_root_two, s * pltpu.roll(s, A - 1, 0), t)
            for i, x in enumerate(blocks):
                hi, lo = split(x)
                if i == 3:
                    lo = (x - hi.astype(F32))
                    lo = jnp.where(row == A - 1, jnp.broadcast_to(free, (A, SUB)), lo).astype(BF16)
                f_ref[i * A : (i + 1) * A, to] = hi
                f_ref[N + i * A : N + (i + 1) * A, to] = lo
            cf = jnp.broadcast_to(cf_ref[:, at], (16, SUB))
            c0 = cf.astype(BF16).astype(F32)
            c1 = (cf - c0).astype(BF16).astype(F32)
            c2 = cf - c0 - c1
            tar_ref[:, at] = jnp.where(
                trow == 0, c0, jnp.where(trow == 1, c1, jnp.where(trow == 2, c2, 0.0))
            ).astype(BF16)

    def gram_dot(c, f_ref, half):
        f = f_ref[:, pl.ds(pl.multiple_of(half * width, width), width)]
        acc[...] += lax.dot_general(f, f, LAST, preferred_element_type=F32)
        at = pl.ds(pl.multiple_of(c * width, width), width)
        acct[...] += lax.dot_general(tar_ref[:, at], f, LAST, preferred_element_type=F32)

    pairs = chunks // 2
    basis(0, fe_ref, 0)

    def gram_step(i, carry):
        basis(2 * i + 1, fo_ref, i)
        gram_dot(2 * i, fe_ref, i)
        basis(2 * i + 2, fe_ref, i + 1)
        gram_dot(2 * i + 1, fo_ref, i)
        return carry

    lax.fori_loop(0, pairs - 1, gram_step, 0)
    basis(chunks - 1, fo_ref, pairs - 1)
    gram_dot(chunks - 2, fe_ref, pairs - 1)
    gram_dot(chunks - 1, fo_ref, pairs - 1)

    low_row = lax.broadcasted_iota(jnp.int32, (N, N), 0) < N - 1
    low_col = lax.broadcasted_iota(jnp.int32, (N, N), 1) < N - 1
    cross = jnp.where(low_col, acc[:N, N:], 0.0) + jnp.where(low_row, acc[N:, :N], 0.0)
    gram = (acc[:N, :N] + cross) + jnp.where(jnp.logical_and(low_row, low_col), acc[N:, N:], 0.0)
    lane1 = lax.broadcasted_iota(jnp.int32, (16, N), 1)
    moment = acct[:, :N] + jnp.where(lane1 < N - 1, acct[:, N:], 0.0)
    lane1 = lax.broadcasted_iota(jnp.int32, (1, N), 1)
    moment_free = acc[2 * N - 1 :, :N] + jnp.where(lane1 < N - 1, acc[2 * N - 1 :, N:], 0.0)
    lane = lax.broadcasted_iota(jnp.int32, (N // 2, N), 1)
    prow = lax.broadcasted_iota(jnp.int32, (N // 2, N), 0)
    corner = pltpu.roll(gram[N // 2 :, :], N // 2, 1)
    packed = jnp.where(lane < prow, corner, gram[: N // 2, :])
    diagonal = jnp.sum(jnp.where(lane == prow, corner, 0.0), axis=0, keepdims=True)
    for j in range(8):
        pay[j] = packed[8 * j : 8 * j + 8, :]
    r8 = lax.broadcasted_iota(jnp.int32, (8, N), 0)
    pay[8] = jnp.where(
        r8 == 0,
        moment[0:1, :] + moment[1:2, :] + moment[2:3, :],
        jnp.where(r8 == 1, moment_free, jnp.where(r8 == 2, diagonal, 0.0)),
    )

    def rs_copy(slot):
        return pltpu.make_async_remote_copy(
            src_ref=pay.at[slot], dst_ref=recv.at[me], send_sem=rs_send.at[slot], recv_sem=rs_recv.at[me],
            device_id=place(slot, my_z), device_id_type=MESH,
        )

    def rs_start(low, high):
        for slot in range(low, high):
            @pl.when(me != slot)
            def _():
                rs_copy(slot).start()

            @pl.when(me == slot)
            def _():
                recv[me] = pay[slot]

    def arrived(buffer, sem, i):
        return pltpu.make_async_remote_copy(
            src_ref=buffer.at[i], dst_ref=buffer.at[i], send_sem=rs_send.at[0], recv_sem=sem.at[i],
            device_id=place(me, my_z), device_id_type=MESH,
        )

    def z_copy(d):
        return pltpu.make_async_remote_copy(
            src_ref=zrecv.at[my_z], dst_ref=zrecv.at[my_z], send_sem=z_send.at[d], recv_sem=z_recv.at[my_z],
            device_id=place(me, (my_z + d) % nz), device_id_type=MESH,
        )

    def ag_copy(slot):
        return pltpu.make_async_remote_copy(
            src_ref=total.at[me], dst_ref=total.at[me], send_sem=ag_send.at[slot], recv_sem=ag_recv.at[me],
            device_id=place(slot, my_z), device_id_type=MESH,
        )

    def z_stage():
        def wait(d, carry):
            arrived(recv, rs_recv, (me + d) % plane).wait_recv()
            return carry

        lax.fori_loop(1, plane, wait, 0)
        parts = [recv[i] for i in range(plane)]
        while len(parts) > 1:
            parts = [parts[i] + parts[i + 1] for i in range(0, len(parts), 2)]
        zrecv[my_z] = parts[0]
        for i in range(nz // 2):
            for d in ((nz // 2,) if i == 0 else (nz // 2 - i, nz // 2 + i)):
                z_copy(d).start()

    def ag_stage():
        def wait(d, carry):
            arrived(zrecv, z_recv, (my_z + d) % nz).wait_recv()
            return carry

        lax.fori_loop(1, nz, wait, 0)
        parts = [zrecv[i] for i in range(nz)]
        while len(parts) > 1:
            parts = [parts[i] + parts[i + 1] for i in range(0, len(parts), 2)]
        total[me] = parts[0]

        for slot in range(plane):
            @pl.when(me != slot)
            def _():
                ag_copy(slot).start()

    def ag_wait(low, high):
        def wait(slot, carry):
            @pl.when(me != slot)
            def _():
                arrived(total, ag_recv, slot).wait_recv()

            return carry

        lax.fori_loop(low, high, wait, 0)

    owns_gram = owns_rest = None
    if comm:
        owns_gram = me < GSLOTS
        owns_rest = jnp.logical_and(me >= GSLOTS, me < SLOTS)
        pl.semaphore_wait(barrier, nz - 1 + plane - 1)
        rs_start(0, GSLOTS)

    accm[...] = jnp.zeros_like(accm)
    accc[...] = jnp.zeros_like(accc)
    accd[...] = jnp.zeros_like(accd)
    accv[...] = jnp.zeros_like(accv)

    def adjoint(c, slot):
        sums = [jnp.zeros((A, SUB), F32) for _ in range(7)]
        for b in range(width // SUB):
            at = pl.ds(pl.multiple_of(c * width + b * SUB, SUB), SUB)
            to = pl.ds(b * SUB, SUB)
            s, t = s_ref[:, at], t_ref[:, at]
            up, down, flat = pltpu.roll(s, A - 1, 0), pltpu.roll(s, 1, 0), 1.0 - t * t
            spread = wide(0)
            e = 1.0 + s * spread
            drift = e * (z_ref[:, at] - spread)
            q = (drift - s) * wide(3)
            cf = cf_ref[:, at]
            for i, x in enumerate(
                (q, q * s, q * up, q * down, q * flat)
            ):
                hi, lo = split(x)
                q_ref[slot, i * A : (i + 1) * A, to] = hi
                q_ref[slot, (5 + i) * A : (6 + i) * A, to] = lo
                sums[i] = sums[i] + x * cf
            basket = jnp.sum(wide(4) * e, axis=0, keepdims=True)
            arg = (basket - 1.0) * (1.0 / soft_width)
            tiny = jnp.exp(-jnp.abs(arg))
            plus = jnp.maximum(arg, 0.0) + jnp.log1p(tiny)
            slope = jnp.where(arg >= 0.0, 1.0, tiny) / (1.0 + tiny)
            taken = 1.0 - free_ref[:, at]
            bar = taken * (notional * slope)
            rew_ref[:, at] = taken * (notional * soft_width * plus)
            bar_ref[:, at] = bar
            sums[5] = sums[5] + bar * (e - basket)
            sums[6] = sums[6] + bar * drift
        for i, x in enumerate(sums):
            folded = x[:, :128]
            for j in range(1, SUB // 128):
                folded = folded + x[:, j * 128 : (j + 1) * 128]
            if i < 5:
                accc[i * A : (i + 1) * A, :] += folded
            else:
                (accd, accv)[i - 5][...] += folded

    def rest_dot(slot, f_ref, half):
        f = f_ref[:, pl.ds(pl.multiple_of(half * width, width), width)]
        accm[...] += lax.dot_general(q_ref[slot], f, LAST, preferred_element_type=F32)

    def adjoint_step(i, carry):
        if comm:
            @pl.when(jnp.logical_and(owns_gram, i == pairs // 2))
            def _():
                z_stage()

        adjoint(2 * i + 1, 1)
        rest_dot(0, fe_ref, i)
        adjoint(2 * i + 2, 0)
        rest_dot(1, fo_ref, i)
        return carry

    adjoint(0, 0)
    lax.fori_loop(0, pairs - 1, adjoint_step, 0)
    adjoint(chunks - 1, 1)
    rest_dot(0, fe_ref, pairs - 1)
    rest_dot(1, fo_ref, pairs - 1)

    lowl = lax.broadcasted_iota(jnp.int32, (5 * A, N), 1) < N - 1
    right = accm[: 5 * A, N:] + accm[5 * A :, N:]
    rest = (accm[: 5 * A, :N] + accm[5 * A :, :N]) + jnp.where(lowl, right, 0.0)
    mfree = right[:, N - 1 : N]
    for j in range(20):
        pay[GSLOTS + j] = rest[8 * j : 8 * j + 8, :]
    lane8 = lax.broadcasted_iota(jnp.int32, (8, N), 1)
    cols = []
    dsum = jnp.sum(accd[...], axis=1, keepdims=True)
    vsum = jnp.sum(accv[...], axis=1, keepdims=True)
    mcf = jnp.sum(accc[...], axis=1, keepdims=True)
    for x, count in ((dsum, 4), (vsum, 4), (mcf, 20), (mfree, 20)):
        cols += [x[8 * i : 8 * i + 8, :] for i in range(count)]
    extra = jnp.zeros((8, N), F32)
    for i, x in enumerate(cols):
        extra = jnp.where(lane8 == i, x, extra)
    pay[SLOTS - 1] = extra

    if comm:
        rs_start(GSLOTS, SLOTS)

    def neighbours(c, carry):
        at = pl.ds(pl.multiple_of(c * 512, 512), 512)
        s, t = s_ref[:, at], t_ref[:, at]
        up_ref[:, at] = pltpu.roll(s, A - 1, 0)
        down_ref[:, at] = pltpu.roll(s, 1, 0)
        flat_ref[:, at] = 1.0 - t * t
        return carry

    lax.fori_loop(0, local // 512, neighbours, 0)

    if comm:

        @pl.when(owns_rest)
        def _():
            z_stage()

        @pl.when(owns_gram)
        def _():
            ag_stage()

        ag_wait(0, GSLOTS)
    else:
        total[...] = pay[...]

    per_path = 1.0 / total_paths
    packed = jnp.concatenate([total[j] for j in range(8)], axis=0)
    upper = jnp.where(lane > prow, packed, jnp.where(lane == prow, 0.5 * packed, 0.0))
    tail = total[8]
    lower = jnp.where(
        lane == prow, 0.5 * jnp.broadcast_to(tail[2:3, :], (N // 2, N)), jnp.where(lane < prow, packed, 0.0)
    )
    lower = pltpu.roll(jnp.where(lane < N // 2, lower, 0.0), N // 2, 1)
    folded = jnp.concatenate([upper, lower], axis=0) * per_path
    gram = folded + folded.T

    def between():
        if comm:
            @pl.when(owns_rest)
            def _():
                ag_stage()

    sol = solve(gram, jnp.where(r8 < 2, tail, 0.0) * per_path, between)
    reg, mult = sol[0:1, :], sol[1:2, :]
    big = lax.broadcasted_iota(jnp.int32, (N, N), 0)
    coef = jnp.where(big == 0, reg, jnp.where(big == 1, mult, 0.0)).T

    offsets = []
    for i in range(2):
        c1, c2, c3, c4 = (coef[A * b : A * (b + 1), i : i + 1] for b in range(4))
        c2 = c2 * inv_root_two
        c3d = jnp.concatenate([c3[A - 1 :], c3[: A - 1]], axis=0)
        for j, x in enumerate((c1, c2, c3, c3d, c4)):
            const[7 + 5 * i + j] = jnp.broadcast_to(x, (A, 128))
        offsets.append(jnp.sum(c2, axis=0, keepdims=True))

    def path_step(c, carry):
        for b in range(width // SUB):
            at = pl.ds(pl.multiple_of(c * width + b * SUB, SUB), SUB)
            s, t = s_ref[:, at], t_ref[:, at]
            up, down, flat = up_ref[:, at], down_ref[:, at], flat_ref[:, at]
            fits, bars = [], []
            for i in range(2):
                square = wide(8 + 5 * i) * s
                lead = wide(7 + 5 * i) + square + wide(9 + 5 * i) * up
                c4 = wide(11 + 5 * i)
                fits.append(jnp.sum(s * lead + c4 * t, axis=0, keepdims=True) - offsets[i])
                bars.append(lead + square + wide(10 + 5 * i) * down + c4 * flat)
            free = free_ref[:, at]
            cont, lam = fits
            value_ref[:, at] = rew_ref[:, at] + free * cont
            flow_ref[:, at] = lam
            cot_ref[:, at] = (
                wide(5) * ((cf_ref[:, at] - cont) * bars[1] + (free - lam) * bars[0]) + wide(6) * bar_ref[:, at]
            )
        return carry

    lax.fori_loop(0, chunks, path_step, 0)

    if comm:
        ag_wait(GSLOTS, SLOTS)
    extra = total[SLOTS - 1]
    vega = [jnp.zeros((8, 1), F32) for _ in range(4)]
    for kind in range(5):
        at = A * (kind if kind < 3 else kind - 1)
        cr, cm = coef[at : at + A, 0:1], coef[at : at + A, 1:2]
        if kind == 3:
            cr = jnp.concatenate([cr[A - 1 :], cr[: A - 1]], axis=0)
            cm = jnp.concatenate([cm[A - 1 :], cm[: A - 1]], axis=0)
        if kind == 1:
            cr, cm = cr * root_two, cm * root_two
        for i in range(4):
            j = 4 * kind + i
            block = total[GSLOTS + j]
            mr = extra[:, 8 + j : 9 + j] - jnp.sum(block * reg, axis=1, keepdims=True)
            mm = extra[:, 28 + j : 29 + j] - jnp.sum(block * mult, axis=1, keepdims=True)
            lo = 8 * i
            vega[i] = vega[i] + cm[lo : lo + 8] * mr + cr[lo : lo + 8] * mm
    delta = weight / whole * jnp.concatenate([extra[:, i : i + 1] for i in range(4)], axis=0)
    vrew = (root_time * share) * jnp.concatenate([extra[:, 4 + i : 5 + i] for i in range(4)], axis=0)
    vega = jnp.concatenate(vega, axis=0) + vrew
    glane = lax.broadcasted_iota(jnp.int32, (A, N), 1)
    both = jnp.where(glane == 0, delta, jnp.where(glane == 1, vega, 0.0)) * per_path
    both = jnp.concatenate([both, jnp.zeros((N - A, N), F32)], axis=0).T
    greek_out[...] = both[0:2, 0:A]

    if comm:
        def sent_slot(slot, carry):
            @pl.when(me != slot)
            def _():
                rs_copy(slot).wait_send()

            return carry

        lax.fori_loop(0, SLOTS, sent_slot, 0)

        @pl.when(me < SLOTS)
        def _():
            def sent_z(d, carry):
                z_copy(d).wait_send()
                return carry

            lax.fori_loop(1, nz, sent_z, 0)

            def sent_ag(slot, carry):
                @pl.when(me != slot)
                def _():
                    ag_copy(slot).wait_send()

                return carry

            lax.fori_loop(0, plane, sent_ag, 0)


def second_kernel(value_ref, cot_ref, flow_ref, greek_ref, value_hbm, cot_hbm, flow_hbm, greek_hbm, sem):
    copies = [(value_ref, value_hbm), (flow_ref, flow_hbm), (greek_ref, greek_hbm)]
    copies = [(cot_ref.at[8 * i : 8 * i + 8], cot_hbm.at[8 * i : 8 * i + 8]) for i in range(A // 8)] + copies
    copies = [pltpu.make_async_copy(src, dst, sem.at[i]) for i, (src, dst) in enumerate(copies)]
    for copy in copies:
        copy.start()
    for copy in copies:
        copy.wait()


def per_device(dims, total_paths, normals, spot, vol, weights, cash_flows, exercise, width=2048):
    comm = dims is not None
    local = normals.shape[1]
    chunks = local // width
    spot, vol, weights = (x.reshape(1, A) for x in (spot, vol, weights))
    cash_flows, exercise = cash_flows.reshape(1, local), exercise.reshape(1, local)
    if comm:
        normals, spot, vol, weights, cash_flows, exercise = (
            pltpu.with_memory_space_constraint(x, pltpu.HBM)
            for x in (normals, spot, vol, weights, cash_flows, exercise)
        )
    vmem = pl.BlockSpec(memory_space=pltpu.VMEM)
    hbm = pl.BlockSpec(memory_space=pltpu.HBM)
    nz, plane = (dims[3], dims[0] * dims[1] * dims[2]) if comm else (2, 2)
    dma = pltpu.SemaphoreType.DMA
    wide, flat = jax.ShapeDtypeStruct((A, local), F32), jax.ShapeDtypeStruct((1, local), F32)
    half = pltpu.VMEM((2 * N, local // 2), BF16)
    tiny = pltpu.VMEM((1, A), F32)
    results = pl.pallas_call(
        functools.partial(first_kernel, dims, total_paths, width),
        out_shape=(flat, wide, flat, jax.ShapeDtypeStruct((2, A), F32)),
        in_specs=[hbm] * 6,
        out_specs=(vmem,) * 4,
        scratch_shapes=[
            *[pltpu.VMEM((A, local), F32)] * 5, *[pltpu.VMEM((1, local), F32)] * 4,
            pltpu.VMEM((A, local), F32), tiny, tiny, tiny, pltpu.VMEM((1, local), jnp.int32),
            half, half, pltpu.VMEM((16, local), BF16), pltpu.VMEM((2, 10 * A, width), BF16),
            pltpu.VMEM((17, A, 128), F32),
            pltpu.VMEM((2 * N, 2 * N), F32), pltpu.VMEM((16, 2 * N), F32),
            pltpu.VMEM((10 * A, 2 * N), F32), pltpu.VMEM((5 * A, 128), F32),
            pltpu.VMEM((A, 128), F32), pltpu.VMEM((A, 128), F32),
            pltpu.VMEM((SLOTS, 8, N), F32), pltpu.VMEM((plane, 8, N), F32),
            pltpu.VMEM((nz, 8, N), F32), pltpu.VMEM((SLOTS, 8, N), F32),
            dma((chunks,)), dma((5,)), dma((SLOTS,)), dma((plane,)),
            dma((nz,)), dma((nz,)), dma((plane,)), dma((SLOTS,)),
        ],
        compiler_params=pltpu.CompilerParams(
            has_side_effects=True, vmem_limit_bytes=40 * 2**20, **({"collective_id": 0} if comm else {})
        ),
        name="normal_equations",
    )(normals, spot, vol, weights, cash_flows, exercise)
    value, cot, flow, greeks = pl.pallas_call(
        second_kernel,
        out_shape=(flat, wide, flat, jax.ShapeDtypeStruct((2, A), F32)),
        in_specs=[vmem] * 4,
        out_specs=(hbm,) * 4,
        scratch_shapes=[dma((A // 8 + 3,))],
        compiler_params=pltpu.CompilerParams(vmem_limit_bytes=4 * 2**20),
        name="put_out",
    )(*results)
    return value.reshape(local), cot, flow.reshape(local), greeks


def solution(mesh):
    shape = dict(mesh.shape)
    ncore, ny = 2, 4
    dims = (shape["grp"] // ncore, ncore, ny, shape["path"] // ny)
    count = shape["grp"] * shape["path"]

    def body(normals, *rest):
        return per_device(dims, normals.shape[1] * count, normals, *rest)

    split_paths = ("grp", "path")
    in_specs = (P(None, split_paths), P(), P(), P(), P(split_paths), P(split_paths))
    out_specs = (P(split_paths), P(None, split_paths), P(split_paths), P())
    return jax.shard_map(body, mesh=mesh, in_specs=in_specs, out_specs=out_specs, check_vma=False)
```
